128 devices in a mesh: row: 8 (over y_lo, z), col: 16 (over x, y_hi, core).
Axes of the slice: x: 4, y: 4 (y_hi: 2, y_lo: 2; y = y_hi * 2 + y_lo), z: 4, core: 2. Of those that a mesh axis runs over, the one named last changes fastest.
Arguments:
- inverse: float32 [16384, 16384], P('row', 'col'), may hold values from -0.0625 to 0.0625
- pattern: int32 [128, 128], P('row', 'col'), may hold values 0 or 1
- factor_first: float32 [16384, 256], P('col'), may hold values from -1.5 to 1.5
- factor_second: float32 [16384, 256], P('col'), may hold values from -1.5 to 1.5
- rows_first: int32 [64], replicated, may hold values from 0 to 127, as said below
- rows_second: int32 [64], replicated, may hold values from 0 to 127, as said below
- coupling: float32 [256, 256], replicated, may hold values from -0.375 to 0.375
- diag_first: float32 [256, 256], replicated, may hold values from -6 to 6
- diag_second: float32 [256, 256], replicated, may hold values from -6 to 6
Outputs:
- panel_one: float32 [16384, 256], P(('row', 'col'))
- panel_two: float32 [16384, 256], P(('row', 'col'))
- block_one: float32 [256, 256], replicated
- block_cross: float32 [256, 256], replicated
- block_two: float32 [256, 256], replicated
The draws below stay inside these ranges and needn't reach their ends.
Inputs may be any that keep to these rules, and one draw needn't show every extreme that they name: `rows_first`: 64 distinct block indices in increasing order; the first block, the block 64 and the last block are always among them. `rows_second`: 64 distinct block indices in increasing order; the first block, the block 64 and the last block are always among them.
All inputs are finite; a program needn't handle non-finite values. No bound on the sum of `pattern` on one device may be relied on, other than what follows from the above.
Results may differ from the reference program's by a relative error of at most 0.000071.
Values sent between devices are 32-bit elements; how exact they have to be, the bound alone decides.
A program may use at most 128 MiB of HBM per device.

```python
import jax
import jax.numpy as jnp
from jax import lax

M = 16384
W = 256
BLK = 128
MB = 128
NB = 64


def chosen_blocks(key, salt):
    middle = MB // 2
    inner = jax.random.permutation(jax.random.fold_in(key, salt), MB - 3)[:NB - 3].astype(jnp.int32) + 1
    inner = jnp.where(inner >= middle, inner + 1, inner)
    picked = jnp.concatenate([jnp.array([0, middle, MB - 1], jnp.int32), inner])
    return jnp.sort(picked)


def draw_rows_first(key, part):
    return chosen_blocks(key, 17)


def draw_rows_second(key, part):
    return chosen_blocks(key, 29)


def touch_ends(result, own_key, least, largest):
    index_at = [jax.random.randint(jax.random.fold_in(own_key, axis), (), 0, length) for axis, length in enumerate(result.shape)]
    longest = result.shape.index(max(result.shape))
    beside = index_at[:longest] + [(index_at[longest] + 1) % result.shape[longest]] + index_at[longest + 1:]
    return result.at[tuple(index_at)].set(least).at[tuple(beside)].set(largest)


def steps_of(key, extent, split, smallest, top_value):
    def one(axis_at, blocks):
        heights = jax.random.uniform(jax.random.fold_in(jax.random.fold_in(key, 6), axis_at), (blocks,), jnp.float32, smallest / len(split), top_value / len(split))
        return jnp.repeat(jnp.exp(heights), extent[axis_at] // blocks).reshape((-1,) + (1,) * (len(extent) - axis_at - 1))

    factor_of = one(*split[0])
    for cut in split[1:]:
        factor_of = factor_of * one(*cut)
    return factor_of


def noise(stream_key, shape, spread, limit, pieces=(), kind=jnp.bfloat16):
    result = spread * jax.random.normal(stream_key, shape, jnp.float32)
    if pieces:
        result = result * steps_of(stream_key, shape, pieces, -0.22, 0.18)
    return jnp.clip(result, -limit, limit).astype(kind)


def setup_inputs(seed: int = 0) -> dict:
    keys = jax.random.split(jax.random.key(seed), 10)
    return {
        "inverse": noise(keys[0], (M, M), (M // 2) ** -0.5, 0.0625, ((0, 8), (1, 16)), jnp.float32),
        "pattern": touch_ends((jax.random.randint(keys[1], (MB, MB), 0, 8) < 5).astype(jnp.int32), jax.random.fold_in(keys[1], 1), 0, 1),
        "factor_first": noise(keys[2], (M, W), 0.25, 1.5, ((0, 16),), jnp.float32),
        "factor_second": noise(keys[3], (M, W), 0.25, 1.5, ((0, 16),), jnp.float32),
        "rows_first": draw_rows_first(jax.random.fold_in(keys[9], 71), 0),
        "rows_second": draw_rows_second(jax.random.fold_in(keys[9], 71), 0),
        "coupling": noise(keys[6], (W, W), W ** -0.5, 0.375, (), jnp.float32),
        "diag_first": noise(keys[7], (W, W), 1.0, 6.0, (), jnp.float32),
        "diag_second": noise(keys[8], (W, W), 1.0, 6.0, (), jnp.float32),
    }


def row_keep(rows_list):
    block_ids = jnp.arange(MB, dtype=jnp.int32)
    hits = jnp.sum((block_ids[:, None] == rows_list[None, :]).astype(jnp.float32), axis=1)
    return jnp.repeat(hits, BLK)


def reference(inverse, pattern, factor_first, factor_second, rows_first, rows_second, coupling, diag_first, diag_second):
    high = lax.Precision.HIGHEST
    masked = (inverse.reshape(MB, BLK, MB, BLK) * pattern.astype(jnp.float32)[:, None, :, None]).reshape(M, M)
    x_one = factor_first * row_keep(rows_first)[:, None]
    x_two = factor_second * row_keep(rows_second)[:, None]
    panel_one = -jnp.dot(masked, x_one, precision=high)
    block_one = diag_first - jnp.dot(x_one.T, panel_one, precision=high)
    panel_two = -(jnp.dot(masked, x_two, precision=high) + jnp.dot(panel_one, coupling, precision=high))
    block_cross = -(jnp.dot(panel_one.T, x_two, precision=high) + jnp.dot(block_one, coupling, precision=high))
    block_two = diag_second - jnp.dot(x_two.T, panel_two, precision=high) - jnp.dot(coupling.T, block_cross, precision=high)
    return (panel_one, panel_two, block_one, block_cross, block_two)
```

```python
import functools

import jax
import jax.numpy as jnp
from jax import lax
from jax.experimental import pallas as pl
from jax.experimental.pallas import tpu as pltpu
from jax.sharding import PartitionSpec as P

MESH = pl.DeviceIdType.MESH
F32 = jnp.float32
BF16 = jnp.bfloat16
BLK = 128
W = 256
XR = 72
NSTEP = 8

CORE = 0
NEAR = CORE + 8
LEG1 = NEAR + 2
LEG2 = LEG1 + 4
YLEG = LEG2 + 8
YF = YLEG + 1
YLEG1 = YF + 4
YLEG2 = YLEG1 + 2
GC = YLEG2 + 4
R1 = GC + 3
R2 = R1 + 48
R3 = R2 + 12
GF = R3 + 48
NMSG = GF + 3
ROUNDS = 3


def split(a):
    hi = a.astype(BF16)
    return hi, (a - hi.astype(F32)).astype(BF16)


def dot3(ah, al, bh, bl, dims=(((1,), (0,)), ((), ()))):
    d = functools.partial(lax.dot_general, dimension_numbers=dims, preferred_element_type=F32)
    return d(ah, bh) + d(al, bh) + d(ah, bl)


def kernel(
    inv_ref, pat_ref, f1_ref, f2_ref, rows1_ref, rows2_ref, coup_ref, d1_ref, d2_ref,
    p1_out, p2_out, b1_out, bc_out, b2_out,
    a, fac, xh, xl, own, give, got, near, nth, ntl, l1, r2, ry, yf, yl1, yr2,
    g, gc, r1, zs, res,
    ssem, rsem, lsem, asem, round_sem,
):
    row, col = lax.axis_index("row"), lax.axis_index("col")
    core = lax.rem(col, 2)
    pos = {"x": col // 4, "y": lax.rem(col // 2, 2) * 2 + row // 4, "z": lax.rem(row, 4)}
    other = 1 - core
    yh = lax.rem(col // 2, 2)

    def device(x, y, z, c):
        return (lax.rem(y, 2) * 4 + z, x * 4 + (y // 2) * 2 + c)

    def at(x=0, y=0, z=0, flip=False):
        return device(
            lax.rem(pos["x"] + x, 4), lax.rem(pos["y"] + y, 4), lax.rem(pos["z"] + z, 4),
            other if flip else core,
        )

    def send(src, dst, k, dev):
        pltpu.make_async_remote_copy(
            src, dst, ssem.at[k], rsem.at[k], device_id=dev, device_id_type=MESH
        ).start()

    me = at()

    def arrived(dst, k):
        pltpu.make_async_remote_copy(
            dst, dst, ssem.at[k], rsem.at[k], device_id=me, device_id_type=MESH
        ).wait_recv()

    def sent(src, k):
        pltpu.make_async_remote_copy(
            src, src, ssem.at[k], rsem.at[k], device_id=me, device_id_type=MESH
        ).wait_send()

    neighbours = [at(x=1), at(x=3), at(y=1), at(y=3), at(z=1), at(z=3)]
    x_up, x_down, y_two, mate = at(x=1), at(x=3), at(y=2), at(flip=True)

    y_lo, z = row // 4, lax.rem(row, 4)
    home = 2 * y_lo + z // 2
    src_z = lax.rem(pos["x"] + 4 - home + z + 1, 4)
    src_dev = device(home, lax.rem(z, 2) * 2 + yh, src_z, pos["x"] // 2)
    to_z = 2 * lax.rem(pos["x"], 2) + yh
    to_x = lax.rem(z + 8 - 1 - to_z + pos["x"], 4)
    to_ylo = pos["x"] // 2
    to_yh = y_lo
    serves = (core == to_x // 2).astype(jnp.int32)

    barrier = pltpu.get_barrier_semaphore()
    for dev in [*neighbours, y_two, mate, src_dev]:
        pl.semaphore_signal(barrier, inc=1, device_id=dev, device_id_type=MESH)

    loads = [
        pltpu.make_async_copy(f1_ref, fac.at[0], lsem.at[0]),
        pltpu.make_async_copy(f2_ref, fac.at[1], lsem.at[1]),
    ]
    for copy in loads:
        copy.start()

    def place(s):
        k = s // 2
        dx = jnp.where(k == 0, 2, jnp.where(k == 1, 1, jnp.where(k == 2, 3, 0)))
        tx = lax.rem(pos["x"] + dx, 4)
        tyh = lax.rem(yh + 1 - lax.rem(s, 2), 2)
        return tx * 2 + tyh

    def load_a(s):
        return pltpu.make_async_copy(
            inv_ref.at[pl.ds(pl.multiple_of(place(s) * 256, 256), 256)], a.at[s], asem.at[s]
        )

    for s in range(NSTEP):
        load_a(s).start()

    def member(rows_ref, first, count):
        ids = lax.broadcasted_iota(jnp.int32, (8, 64), 0) + first
        hits = (ids == rows_ref[...].reshape(1, 64)).astype(F32)
        return jnp.sum(hits, axis=1, keepdims=True)[:count]

    pl.semaphore_wait(barrier, 8 + 2 * serves)

    for copy in loads:
        copy.wait()

    @pl.when(serves == 1)
    def _():
        for c in range(2):
            block = lax.rem(to_x, 2) * 4 + to_yh * 2 + c
            rows = pl.ds(pl.multiple_of(block * BLK, BLK), BLK)
            pltpu.make_async_remote_copy(
                fac.at[:, rows], near, ssem.at[NEAR + c], rsem.at[NEAR],
                device_id=device(to_x, to_yh * 2 + to_ylo, to_z, c), device_id_type=MESH,
            ).start()

    for p, rows_ref in enumerate((rows1_ref, rows2_ref)):
        keep = member(rows_ref, col * 8, 8)
        for j in range(8):
            rows = slice(j * BLK, (j + 1) * BLK)
            hi, lo = split(fac[p, rows, :] * keep[j : j + 1, :])
            xh[rows, p * W : (p + 1) * W] = hi
            xl[rows, p * W : (p + 1) * W] = lo

    for dev in neighbours:
        pl.semaphore_signal(round_sem.at[0], inc=1, device_id=dev, device_id_type=MESH)

    def compute(s):
        load_a(s).wait()
        base = place(s) * 2
        parts = []
        for half in (other, core):
            r0 = pl.multiple_of(half * BLK, BLK)
            parts.append(
                jnp.concatenate(
                    [
                        a[s, pl.ds(r0, BLK), j * BLK : (j + 1) * BLK]
                        * pat_ref[base + half, j].astype(F32)
                        for j in range(8)
                    ],
                    axis=1,
                )
            )
        ah, al = split(jnp.concatenate(parts, axis=0))
        out = dot3(ah, al, xh[...], xl[...])
        for p in range(2):
            give[s, p] = out[:BLK, p * W : (p + 1) * W]
            own[s, p] = out[BLK:, p * W : (p + 1) * W]
        send(give.at[s], got.at[s], CORE + s, mate)

    lo_rows, hi_rows = pl.ds(0, XR), pl.ds(XR, BLK - XR)

    def fold(s):
        arrived(got.at[s], CORE + s)
        own[s] += got[s]

    def after(s):
        k, w = s // 2, s % 2
        if k == 0:
            send(own.at[s, 0, lo_rows], l1.at[w, 0], LEG1 + 2 * w, x_up)
            send(own.at[s, 1, lo_rows], l1.at[w, 1], LEG1 + 2 * w + 1, x_down)
        elif k == 1:
            send(own.at[s, 1, lo_rows], r2.at[w, 0, 1], LEG2 + 4 * w + 1, x_up)
        elif k == 2:
            send(own.at[s, 0, lo_rows], r2.at[w, 1, 0], LEG2 + 4 * w + 2, x_down)
        if w == 0:
            send(own.at[s, :, hi_rows], yf.at[k], YF + k, y_two)

    def relay(w):
        for d, s, dev in ((0, 2 + w, x_up), (1, 4 + w, x_down)):
            arrived(l1.at[w, d], LEG1 + 2 * w + d)
            own[s, d, :XR] += l1[w, d]
            send(own.at[s, d, lo_rows], r2.at[w, d, d], LEG2 + 4 * w + 2 * d + d, dev)

    def fold_y(k):
        arrived(yf.at[k], YF + k)
        own[2 * k + 1, :, XR:] += yf[k]

    def step(s, carry):
        compute(s)
        for t in range(NSTEP - 1):

            @pl.when(s == t + 1)
            def _(t=t):
                fold(t)
                after(t)
                if t == 4:
                    relay(0)
                if t == 6:
                    relay(1)

            if 1 <= t <= ROUNDS:

                @pl.when(s == t + 1)
                def _(t=t):
                    pl.semaphore_wait(round_sem.at[t - 1], 6)
                    if t < ROUNDS:
                        for dev in neighbours:
                            pl.semaphore_signal(
                                round_sem.at[t], inc=1, device_id=dev, device_id_type=MESH
                            )

        return carry

    lax.fori_loop(0, NSTEP, step, 0)
    fold(7)

    fold_y(0)
    send(own.at[1, 0, hi_rows], yl1.at[0], YLEG1, x_up)
    send(own.at[1, 1, hi_rows], yl1.at[1], YLEG1 + 1, x_down)

    small = [
        pltpu.make_async_copy(coup_ref, res.at[3], lsem.at[0]),
        pltpu.make_async_copy(d1_ref, res.at[4], lsem.at[1]),
        pltpu.make_async_copy(d2_ref, res.at[5], lsem.at[2]),
    ]
    for copy in small:
        copy.start()
    arrived(near, NEAR)
    own_id = row * 16 + col
    for p, rows_ref in enumerate((rows1_ref, rows2_ref)):
        keep = member(rows_ref, own_id, 1)
        hi, lo = split((near[p] * keep).T)
        nth[p], ntl[p] = hi, lo
    for copy in small:
        copy.wait()

    fold_y(1)
    send(own.at[3, 1, hi_rows], yr2.at[0, 1], YLEG2 + 1, x_up)
    fold_y(2)
    send(own.at[5, 0, hi_rows], yr2.at[1, 0], YLEG2 + 2, x_down)

    for d in range(2):
        for p in range(2):
            arrived(r2.at[0, d, p], LEG2 + 2 * d + p)
    own[6, :, :XR] += r2[0, 0] + r2[0, 1]
    send(own.at[6, :, lo_rows], ry, YLEG, y_two)

    for d, s, dev in ((0, 3, x_up), (1, 5, x_down)):
        arrived(yl1.at[d], YLEG1 + d)
        own[s, d, XR:] += yl1[d]
        send(own.at[s, d, hi_rows], yr2.at[d, d], YLEG2 + 2 * d + d, dev)
    fold_y(3)

    for d in range(2):
        for p in range(2):
            arrived(r2.at[1, d, p], LEG2 + 4 + 2 * d + p)
    own[7, :, :XR] += r2[1, 0] + r2[1, 1]
    for d in range(2):
        for p in range(2):
            arrived(yr2.at[d, p], YLEG2 + 2 * d + p)
    own[7, :, XR:] += yr2[0] + yr2[1]
    arrived(ry, YLEG)
    own[7, :, :XR] += ry[...]

    m1, m2 = own[7, 0], own[7, 1]
    m1h, m1l = split(m1)
    ch, cl = split(res[3])
    p2 = dot3(m1h, m1l, ch, cl) - m2
    p1_out[...] = -m1
    p2_out[...] = p2
    p2h, p2l = split(p2)
    m1t_h, m1t_l = split(m1.T)
    g[0] = dot3(nth[0], ntl[0], m1h, m1l)
    n2h, n2l = split(near[1] * member(rows2_ref, own_id, 1))
    g[1] = dot3(m1t_h, m1t_l, n2h, n2l)
    g[2] = dot3(nth[1], ntl[1], p2h, p2l)

    mine, theirs = pl.multiple_of(core * BLK, BLK), pl.multiple_of(other * BLK, BLK)
    half = pl.ds(mine, BLK)
    for m in range(3):
        send(g.at[m, pl.ds(theirs, BLK)], gc.at[m], GC + m, mate)

    planes = (("x", "y", "z"), ("y", "z", "x"), ("z", "x", "y"))

    def shifted(m, i, j, k):
        return at(**dict(zip(planes[m], (i, j, k))))

    def piece(m, i, j):
        u, v, _ = planes[m]
        index = lax.rem(pos[u] + i, 4) * 4 + lax.rem(pos[v] + j, 4)
        return pl.ds(pl.multiple_of(mine + index * 8, 8), 8)

    order = sorted(
        ((i, j) for i in range(4) for j in range(4) if (i, j) != (0, 0)),
        key=lambda q: -(min(q[0], 4 - q[0]) + min(q[1], 4 - q[1])),
    )
    for m in range(3):
        arrived(gc.at[m], GC + m)
        g[m, half] += gc[m]
        for i, j in order:
            q = i * 4 + j
            send(g.at[m, piece(m, i, j)], r1.at[m, q], R1 + 16 * m + q, shifted(m, i, j, 0))
    for m in range(3):
        total = g[m, piece(m, 0, 0)]
        for i, j in reversed(order):
            q = i * 4 + j
            arrived(r1.at[m, q], R1 + 16 * m + q)
            total += r1[m, q]
        slot = pos[planes[m][2]]
        zs[m, slot] = total
        for k in (2, 1, 3):
            send(zs.at[m, slot], zs.at[m, slot], R2 + 4 * m + k, shifted(m, 0, 0, k))
    for m in range(3):
        for k in (1, 3, 2):
            slot = lax.rem(pos[planes[m][2]] + 4 - k, 4)
            arrived(zs.at[m, slot], R2 + 4 * m + k)
        res[m, piece(m, 0, 0)] = (zs[m, 0] + zs[m, 1]) + (zs[m, 2] + zs[m, 3])
        for i, j in order:
            q = i * 4 + j
            send(res.at[m, piece(m, 0, 0)], res.at[m, piece(m, 0, 0)], R3 + 16 * m + q, shifted(m, i, j, 0))
    for m in range(3):
        for i, j in reversed(order):
            q = i * 4 + j
            arrived(res.at[m, piece(m, 4 - i, 4 - j)], R3 + 16 * m + q)
        send(res.at[m, half], res.at[m, half], GF + m, mate)
    for m in range(3):
        arrived(res.at[m, pl.ds(theirs, BLK)], GF + m)

    b1 = res[4] + res[0]
    b1h, b1l = split(b1)
    bc = res[1] - dot3(b1h, b1l, ch, cl)
    bch, bcl = split(bc)
    cth, ctl = split(res[3].T)
    b1_out[...] = b1
    bc_out[...] = bc
    b2_out[...] = res[5] - res[2] - dot3(cth, ctl, bch, bcl)

    for s in range(NSTEP):
        sent(give.at[s], CORE + s)

    @pl.when(serves == 1)
    def _():
        for c in range(2):
            sent(near, NEAR + c)

    for k in range(4):
        sent(l1.at[0, 0], LEG1 + k)
    for k in range(8):
        sent(l1.at[0, 0], LEG2 + k)
    sent(ry, YLEG)
    for k in range(4):
        sent(yf.at[0], YF + k)
        sent(yl1.at[0], YLEG2 + k)
    for k in range(2):
        sent(yl1.at[0], YLEG1 + k)
    for m in range(3):
        sent(gc.at[m], GC + m)
        sent(gc.at[m], GF + m)
        for q in range(1, 16):
            sent(r1.at[m, q], R1 + 16 * m + q)
            sent(r1.at[m, q], R3 + 16 * m + q)
        for k in range(1, 4):
            sent(r1.at[m, 0], R2 + 4 * m + k)


def per_device(inverse, pattern, first, second, rows1, rows2, coupling, diag1, diag2):
    any_, vmem, smem = (
        pl.BlockSpec(memory_space=pl.ANY),
        pl.BlockSpec(memory_space=pltpu.VMEM),
        pl.BlockSpec(memory_space=pltpu.SMEM),
    )
    V = pltpu.VMEM
    return pl.pallas_call(
        kernel,
        out_shape=[jax.ShapeDtypeStruct((BLK, W), F32)] * 2 + [jax.ShapeDtypeStruct((W, W), F32)] * 3,
        in_specs=[any_, smem, any_, any_, vmem, vmem, any_, any_, any_],
        out_specs=[vmem] * 5,
        scratch_shapes=[
            V((8, 256, 1024), F32),
            V((2, 1024, W), F32),
            V((1024, 2 * W), BF16),
            V((1024, 2 * W), BF16),
            V((8, 2, BLK, W), F32),
            V((8, 2, BLK, W), F32),
            V((8, 2, BLK, W), F32),
            V((2, BLK, W), F32),
            V((2, W, BLK), BF16),
            V((2, W, BLK), BF16),
            V((2, 2, XR, W), F32),
            V((2, 2, 2, XR, W), F32),
            V((2, XR, W), F32),
            V((4, 2, BLK - XR, W), F32),
            V((2, BLK - XR, W), F32),
            V((2, 2, BLK - XR, W), F32),
            V((3, W, W), F32),
            V((3, BLK, W), F32),
            V((3, 16, 8, W), F32),
            V((3, 4, 8, W), F32),
            V((6, W, W), F32),
            pltpu.SemaphoreType.DMA((NMSG,)),
            pltpu.SemaphoreType.DMA((NMSG,)),
            pltpu.SemaphoreType.DMA((3,)),
            pltpu.SemaphoreType.DMA((8,)),
            pltpu.SemaphoreType.REGULAR((ROUNDS,)),
        ],
        compiler_params=pltpu.CompilerParams(
            collective_id=0, has_side_effects=True, vmem_limit_bytes=62 * 2**20
        ),
    )(inverse, pattern, first, second, rows1, rows2, coupling, diag1, diag2)


def solution(mesh):
    return jax.shard_map(
        per_device,
        mesh=mesh,
        in_specs=(
            P("row", "col"), P("row", "col"), P("col", None), P("col", None),
            P(), P(), P(), P(), P(),
        ),
        out_specs=(P(("row", "col"), None), P(("row", "col"), None), P(), P(), P()),
        check_vma=False,
    )
```

```python
import functools

import jax
import jax.numpy as jnp
from jax import lax
from jax.experimental import pallas as pl
from jax.experimental.pallas import tpu as pltpu
from jax.sharding import PartitionSpec as P

MESH = pl.DeviceIdType.MESH
F32 = jnp.float32
BF16 = jnp.bfloat16
BLK = 128
W = 256
XR = 64
YR = BLK - XR
NSTEP = 8
SLOT = {"2o": 0, "2w": 1, "1o": 2, "3o": 3, "1w": 4, "3w": 5, "0o": 6, "0w": 7}

CORE = 0
NEAR = CORE + 8
LEG1 = NEAR + 1
LEG2 = LEG1 + 4
YLEG = LEG2 + 2
YF = YLEG + 1
YLEG1 = YF + 4
YLEG2 = YLEG1 + 2
GC = YLEG2 + 1
R1 = GC + 3
R2 = R1 + 3
R3 = R2 + 3
GF = R3 + 3
NSEM = GF + 3
ROUNDS = 3


def split(a):
    hi = a.astype(BF16)
    return hi, (a - hi.astype(F32)).astype(BF16)


def dot3(a, b):
    d = functools.partial(jnp.dot, preferred_element_type=F32)
    (ah, al), (bh, bl) = a, b
    return d(ah, bh) + d(al, bh) + d(ah, bl)


def join(parts, axis):
    return tuple(jnp.concatenate(p, axis=axis) for p in zip(*parts))


def kernel(
    inv_ref, pat_ref, f1_ref, f2_ref, rows1_ref, rows2_ref, coup_ref, d1_ref, d2_ref,
    p1_out, p2_out, b1_out, bc_out, b2_out,
    a, fac, xh, xl, own, give, got, near, nt, nn, l1, r2, ry, yf, yl1, yr2,
    g, gc, r1, zs, res, const, pan, csp,
    ssem, rsem, lsem, asem, round_sem,
):
    row, col = lax.axis_index("row"), lax.axis_index("col")
    core = lax.rem(col, 2)
    y_lo, z, yh = row // 4, lax.rem(row, 4), lax.rem(col // 2, 2)
    pos = {"x": col // 4, "y": yh * 2 + y_lo, "z": z}
    other = 1 - core

    def device(x, y, z, c):
        return (lax.rem(y, 2) * 4 + z, x * 4 + (y // 2) * 2 + c)

    def at(x=0, y=0, z=0, flip=False):
        return device(
            lax.rem(pos["x"] + x, 4), lax.rem(pos["y"] + y, 4), lax.rem(pos["z"] + z, 4),
            other if flip else core,
        )

    def send(src, dst, k, dev):
        pltpu.make_async_remote_copy(
            src, dst, ssem.at[k], rsem.at[k], device_id=dev, device_id_type=MESH
        ).start()

    me = at()

    def arrived(dst, k):
        pltpu.make_async_remote_copy(
            dst, dst, ssem.at[k], rsem.at[k], device_id=me, device_id_type=MESH
        ).wait_recv()

    def sent(src, k):
        pltpu.make_async_remote_copy(
            src, src, ssem.at[k], rsem.at[k], device_id=me, device_id_type=MESH
        ).wait_send()

    neighbours = [at(x=1), at(x=3), at(y=1), at(y=3), at(z=1), at(z=3)]
    x_up, x_down, y_two, mate = at(x=1), at(x=3), at(y=2), at(flip=True)

    barrier = pltpu.get_barrier_semaphore()
    for dev in [*neighbours, y_two, mate]:
        pl.semaphore_signal(barrier, inc=1, device_id=dev, device_id_type=MESH)

    loads = [
        pltpu.make_async_copy(f1_ref, fac.at[0], lsem.at[0]),
        pltpu.make_async_copy(f2_ref, fac.at[1], lsem.at[1]),
    ]
    for copy in loads:
        copy.start()

    def place(s):
        dx = jnp.where(s < 2, 2, jnp.where(s > 5, 0, 1 + 2 * lax.rem(s, 2)))
        same = jnp.where((s == 1) | (s == 4) | (s == 5) | (s == 7), 1, 0)
        return lax.rem(pos["x"] + dx, 4) * 2 + lax.rem(yh + 1 + same, 2)

    def load_a(s):
        return pltpu.make_async_copy(
            inv_ref.at[pl.ds(pl.multiple_of(place(s) * 256, 256), 256)], a.at[s], asem.at[s]
        )

    for s in range(NSTEP):
        load_a(s).start()
    small = [
        pltpu.make_async_copy(coup_ref, csp, lsem.at[2]),
        pltpu.make_async_copy(d1_ref, const.at[0], lsem.at[3]),
        pltpu.make_async_copy(d2_ref, const.at[2], lsem.at[4]),
    ]
    for copy in small:
        copy.start()

    def member(rows_ref, first, count):
        ids = lax.broadcasted_iota(jnp.int32, (8, 64), 0) + first
        hits = (ids == rows_ref[...].reshape(1, 64)).astype(F32)
        return jnp.sum(hits, axis=1, keepdims=True)[:count]

    for p, rows_ref in enumerate((rows1_ref, rows2_ref)):
        keep = member(rows_ref, col * 8, 8)
        loads[p].wait()
        for j in range(8):
            rows = slice(j * BLK, (j + 1) * BLK)
            hi, lo = split(fac[p, rows, :] * keep[j : j + 1, :])
            xh[rows, p * W : (p + 1) * W] = hi
            xl[rows, p * W : (p + 1) * W] = lo

    to_ylo = pos["x"] // 2
    to_z = 2 * lax.rem(pos["x"], 2) + yh
    to_x = lax.rem(pos["x"] + 2 + to_z + 4 - z, 4)
    to_yh = jnp.where(to_ylo == y_lo, yh, 1 - yh)
    serves = core == to_x // 2

    def send_near():
        @pl.when(serves)
        def _():
            for c in range(2):
                block = lax.rem(to_x, 2) * 4 + to_yh * 2 + c
                rows = pl.ds(pl.multiple_of(block * BLK, BLK), BLK)
                send(fac.at[:, rows], near, NEAR, device(to_x, to_yh * 2 + to_ylo, to_z, c))

    def compute(s):
        load_a(s).wait()
        base = place(s) * 2
        parts = []
        for half in (other, core):
            r0 = pl.multiple_of(half * BLK, BLK)
            parts.append(
                jnp.concatenate(
                    [
                        a[s, pl.ds(r0, BLK), j * BLK : (j + 1) * BLK]
                        * pat_ref[j, base + half].astype(F32)
                        for j in range(8)
                    ],
                    axis=1,
                )
            )
        out = dot3(split(jnp.concatenate(parts, axis=0)), (xh[...], xl[...]))
        for p in range(2):
            give[s, p] = out[:BLK, p * W : (p + 1) * W]
            own[s, p] = out[BLK:, p * W : (p + 1) * W]

    lo_rows, hi_rows = pl.ds(0, XR), pl.ds(XR, YR)

    def fold(s):
        arrived(got.at[s], CORE + s)
        own[s] += got[s]

    def leg1(w, s):
        send(own.at[s, 0, lo_rows], l1.at[w, 0], LEG1 + 2 * w, x_up)
        send(own.at[s, 1, lo_rows], l1.at[w, 1], LEG1 + 2 * w + 1, x_down)

    def leg2_up(w, s):
        send(own.at[s, 1, lo_rows], r2.at[w, 0, 1], LEG2 + w, x_up)

    def leg2_down(w, s):
        send(own.at[s, 0, lo_rows], r2.at[w, 1, 0], LEG2 + w, x_down)

    def relay(w, up, down):
        for d, s, dev in ((0, up, x_up), (1, down, x_down)):
            arrived(l1.at[w, d], LEG1 + 2 * w + d)
            own[s, d, :XR] += l1[w, d]
            send(own.at[s, d, lo_rows], r2.at[w, d, d], LEG2 + w, dev)

    def give_y(dx, s):
        send(own.at[s, :, hi_rows], yf.at[dx], YF + dx, y_two)

    def fold_y(dx, s):
        arrived(yf.at[dx], YF + dx)
        own[s, :, XR:] += yf[dx]

    def hear(k):
        pl.semaphore_wait(round_sem.at[k], 6)

    def tell(k):
        for dev in neighbours:
            pl.semaphore_signal(round_sem.at[k], inc=1, device_id=dev, device_id_type=MESH)

    def after(t):
        if t == 0:
            leg1(0, 0)
            give_y(2, 0)
        elif t == 1:
            leg1(1, 1)
            hear(0)
            tell(1)
        elif t == 2:
            leg2_up(0, 2)
            give_y(1, 2)
        elif t == 3:
            leg2_down(0, 3)
            give_y(3, 3)
            relay(0, 2, 3)
            hear(1)
            tell(2)
        elif t == 4:
            leg2_up(1, 4)
        elif t == 5:
            leg2_down(1, 5)
            hear(2)
            send_near()
            relay(1, 4, 5)
        elif t == 6:
            give_y(0, 6)
            fold_y(2, 1)
            send(own.at[1, 0, hi_rows], yl1.at[0], YLEG1, x_up)
            send(own.at[1, 1, hi_rows], yl1.at[1], YLEG1 + 1, x_down)

    def step(s, carry):
        compute(s)

        @pl.when(s == 0)
        def _():
            pl.semaphore_wait(barrier, 8)
            tell(0)

        send(give.at[s], got.at[s], CORE + s, mate)
        for t in range(NSTEP - 1):

            @pl.when(s == t + 1)
            def _(t=t):
                fold(t)
                after(t)

        return carry

    lax.fori_loop(0, NSTEP, step, 0)
    fold(7)

    arrived(r2.at[0], LEG2)
    own[6, :, :XR] += r2[0, 0] + r2[0, 1]
    send(own.at[6, :, lo_rows], ry, YLEG, y_two)

    def second_leg(d, dx, s, dev):
        fold_y(dx, s)
        send(own.at[s, 1 - d, hi_rows], yr2.at[d, 1 - d], YLEG2, dev)
        arrived(yl1.at[d], YLEG1 + d)
        own[s, d, XR:] += yl1[d]
        send(own.at[s, d, hi_rows], yr2.at[d, d], YLEG2, dev)

    second_leg(0, 1, 4, x_up)

    for copy in small:
        copy.wait()
    coup = csp[...]
    c_split, ct_split = split(coup), split(coup.T)
    d1c = dot3(split(const[0]), c_split)
    const[1] = -d1c
    const[2] += dot3(ct_split, split(d1c))

    second_leg(1, 3, 5, x_down)

    arrived(near, NEAR)
    own_id = row * 16 + col
    n1 = near[0] * member(rows1_ref, own_id, 1)
    n2 = near[1] * member(rows2_ref, own_id, 1)
    n1c = dot3(split(n1), c_split)
    for k, v in enumerate((n1, n2, n1c)):
        nt[0, k], nt[1, k] = split(v.T)
    nn[0], nn[1] = split(n2)

    fold_y(0, 7)
    arrived(r2.at[1], LEG2 + 1)
    own[7, :, :XR] += r2[1, 0] + r2[1, 1]
    arrived(yr2, YLEG2)
    own[7, :, XR:] += yr2[0] + yr2[1]
    arrived(ry, YLEG)
    own[7, :, :XR] += ry[...]

    mine, theirs = pl.multiple_of(core * BLK, BLK), pl.multiple_of(other * BLK, BLK)
    half = pl.ds(mine, BLK)

    def put(m, value):
        g[m] = value
        send(g.at[m, pl.ds(theirs, BLK)], gc.at[m], GC + m, mate)

    m1, m2 = own[7, 0], own[7, 1]
    m1s, m1t = split(m1), split(m1.T)
    n1t, n2t, n1ct = ((nt[0, k], nt[1, k]) for k in range(3))
    n2s = (nn[0], nn[1])
    put(0, dot3(n1t, m1s))
    mc = dot3(m1s, c_split)
    mcs = split(mc)
    minus = lambda v: tuple(-u for u in v)
    put(1, dot3(join((m1t, n1t), 1), join((n2s, minus(mcs)), 0)))
    p2 = mc - m2
    put(2, dot3(join((n2t, split(mc.T), n1ct), 1), join((split(-p2), minus(n2s), mcs), 0)))
    pan[0] = -m1
    pan[1] = p2
    outs = [
        pltpu.make_async_copy(pan.at[0], p1_out, lsem.at[0]),
        pltpu.make_async_copy(pan.at[1], p2_out, lsem.at[1]),
    ]
    for copy in outs:
        copy.start()

    planes = (("x", "y", "z"), ("y", "z", "x"), ("z", "x", "y"))

    def shifted(m, i, j, k):
        return at(**dict(zip(planes[m], (i, j, k))))

    def piece(m, i, j):
        u, v, _ = planes[m]
        index = lax.rem(pos[u] + i, 4) * 4 + lax.rem(pos[v] + j, 4)
        return pl.ds(pl.multiple_of(mine + index * 8, 8), 8)

    order = sorted(
        ((i, j) for i in range(4) for j in range(4) if (i, j) != (0, 0)),
        key=lambda q: -(min(q[0], 4 - q[0]) + min(q[1], 4 - q[1])),
    )
    for m in range(3):
        arrived(gc.at[m], GC + m)
        g[m, half] += gc[m]
        for i, j in order:
            send(g.at[m, piece(m, i, j)], r1.at[m, i * 4 + j], R1 + m, shifted(m, i, j, 0))
    for m in range(3):
        arrived(r1.at[m, 1:16], R1 + m)
        total = g[m, piece(m, 0, 0)]
        for q in range(1, 16):
            total += r1[m, q]
        slot = pos[planes[m][2]]
        zs[m, slot] = total
        for k in (2, 1, 3):
            send(zs.at[m, slot], zs.at[m, slot], R2 + m, shifted(m, 0, 0, k))
    for m in range(3):
        arrived(zs.at[m, 1:4], R2 + m)
        at_piece = piece(m, 0, 0)
        res[m, at_piece] = const[m, at_piece] + ((zs[m, 0] + zs[m, 1]) + (zs[m, 2] + zs[m, 3]))
        for i, j in order:
            send(res.at[m, at_piece], res.at[m, at_piece], R3 + m, shifted(m, i, j, 0))
    for m in range(3):
        arrived(res.at[m, 0:120], R3 + m)
        send(res.at[m, half], res.at[m, half], GF + m, mate)
    for m, out in enumerate((b1_out, bc_out, b2_out)):
        arrived(res.at[m, pl.ds(theirs, BLK)], GF + m)
        outs.append(pltpu.make_async_copy(res.at[m], out, lsem.at[2 + m]))
        outs[-1].start()

    for s in range(NSTEP):
        sent(give.at[s], CORE + s)

    @pl.when(serves)
    def _():
        sent(fac.at[:, 0 : 2 * BLK], NEAR)

    for k in range(4):
        sent(l1.at[0, 0], LEG1 + k)
        sent(yf.at[0], YF + k)
    for k in range(2):
        sent(r2.at[k], LEG2 + k)
        sent(yl1.at[0], YLEG1 + k)
    sent(ry, YLEG)
    sent(yr2, YLEG2)
    for m in range(3):
        sent(gc.at[m], GC + m)
        sent(r1.at[m, 1:16], R1 + m)
        sent(r1.at[m, 1:4], R2 + m)
        sent(r1.at[m, 1:16], R3 + m)
        sent(gc.at[m], GF + m)
    for copy in outs:
        copy.wait()


def per_device(inverse, pattern, first, second, rows1, rows2, coupling, diag1, diag2):
    any_, vmem, smem = (
        pl.BlockSpec(memory_space=pl.ANY),
        pl.BlockSpec(memory_space=pltpu.VMEM),
        pl.BlockSpec(memory_space=pltpu.SMEM),
    )
    V = pltpu.VMEM
    outs = pl.pallas_call(
        kernel,
        out_shape=[jax.ShapeDtypeStruct((BLK, W), F32)] * 2 + [jax.ShapeDtypeStruct((W, W), F32)] * 3,
        in_specs=[any_, smem, any_, any_, vmem, vmem, any_, any_, any_],
        out_specs=[any_] * 5,
        scratch_shapes=[
            V((8, 256, 1024), F32),
            V((2, 1024, W), F32),
            V((1024, 2 * W), BF16),
            V((1024, 2 * W), BF16),
            V((8, 2, BLK, W), F32),
            V((8, 2, BLK, W), F32),
            V((8, 2, BLK, W), F32),
            V((2, BLK, W), F32),
            V((2, 3, W, BLK), BF16),
            V((2, BLK, W), BF16),
            V((2, 2, XR, W), F32),
            V((2, 2, 2, XR, W), F32),
            V((2, XR, W), F32),
            V((4, 2, YR, W), F32),
            V((2, YR, W), F32),
            V((2, 2, YR, W), F32),
            V((3, W, W), F32),
            V((3, BLK, W), F32),
            V((3, 16, 8, W), F32),
            V((3, 4, 8, W), F32),
            V((3, W, W), F32),
            V((3, W, W), F32),
            V((2, BLK, W), F32),
            V((W, W), F32),
            pltpu.SemaphoreType.DMA((NSEM,)),
            pltpu.SemaphoreType.DMA((NSEM,)),
            pltpu.SemaphoreType.DMA((5,)),
            pltpu.SemaphoreType.DMA((8,)),
            pltpu.SemaphoreType.REGULAR((ROUNDS,)),
        ],
        compiler_params=pltpu.CompilerParams(
            collective_id=0, has_side_effects=True, vmem_limit_bytes=62 * 2**20
        ),
    )(inverse, pattern.T, first, second, rows1, rows2, coupling, diag1, diag2)
    return pl.pallas_call(
        hand_over,
        out_shape=[jax.ShapeDtypeStruct(o.shape, o.dtype) for o in outs],
        in_specs=[vmem] * 5,
        out_specs=[any_] * 5,
        scratch_shapes=[pltpu.SemaphoreType.DMA((5,))],
    )(*outs)


def hand_over(*refs):
    sem = refs[-1]
    copies = [pltpu.make_async_copy(refs[i], refs[5 + i], sem.at[i]) for i in range(5)]
    for copy in copies:
        copy.start()
    for copy in copies:
        copy.wait()


def solution(mesh):
    return jax.shard_map(
        per_device,
        mesh=mesh,
        in_specs=(
            P("row", "col"), P("row", "col"), P("col", None), P("col", None),
            P(), P(), P(), P(), P(),
        ),
        out_specs=(P(("row", "col"), None), P(("row", "col"), None), P(), P(), P()),
        check_vma=False,
    )
```

```python
import functools

import jax
import jax.numpy as jnp
from jax import lax
from jax.experimental import pallas as pl
from jax.experimental.pallas import tpu as pltpu
from jax.sharding import PartitionSpec as P

MESH = pl.DeviceIdType.MESH
F32 = jnp.float32
BF16 = jnp.bfloat16
BLK = 128
W = 256
XR = 64
YR = BLK - XR
NSTEP = 8
SLOT = {"2o": 0, "2w": 1, "1o": 2, "3o": 3, "1w": 4, "3w": 5, "0o": 6, "0w": 7}

CORE = 0
NEAR = CORE + 8
LEG1 = NEAR + 1
LEG2 = LEG1 + 4
YLEG = LEG2 + 2
YF = YLEG + 1
YLEG1 = YF + 4
YLEG2 = YLEG1 + 2
GC = YLEG2 + 1
R1 = GC + 3
R2 = R1 + 3
R3 = R2 + 3
GF = R3 + 3
NSEM = GF + 3
ROUNDS = 3


def split(a):
    hi = a.astype(BF16)
    return hi, (a - hi.astype(F32)).astype(BF16)


def dot3(a, b):
    d = functools.partial(jnp.dot, preferred_element_type=F32)
    (ah, al), (bh, bl) = a, b
    return d(ah, bh) + d(al, bh) + d(ah, bl)


def join(parts, axis):
    return tuple(jnp.concatenate(p, axis=axis) for p in zip(*parts))


def kernel(
    inv_ref, pat_hbm, f1_ref, f2_ref, rows1_hbm, rows2_hbm, coup_ref, d1_ref, d2_ref,
    p1_out, p2_out, b1_out, bc_out, b2_out,
    a, fac, xh, xl, own, give, got, near, nt, nn, l1, r2, ry, yf, yl1, yr2,
    g, gc, r1, zs, res, const, csp, rows1_ref, rows2_ref, pat_ref,
    ssem, rsem, lsem, asem, round_sem,
):
    loads = [
        pltpu.make_async_copy(f1_ref, fac.at[0], lsem.at[0]),
        pltpu.make_async_copy(f2_ref, fac.at[1], lsem.at[1]),
    ]
    tiny = [
        pltpu.make_async_copy(rows1_hbm, rows1_ref, lsem.at[5]),
        pltpu.make_async_copy(rows2_hbm, rows2_ref, lsem.at[6]),
        pltpu.make_async_copy(pat_hbm, pat_ref, lsem.at[7]),
    ]
    for copy in tiny + loads:
        copy.start()

    row, col = lax.axis_index("row"), lax.axis_index("col")
    core = lax.rem(col, 2)
    y_lo, z, yh = row // 4, lax.rem(row, 4), lax.rem(col // 2, 2)
    pos = {"x": col // 4, "y": yh * 2 + y_lo, "z": z}
    other = 1 - core

    def device(x, y, z, c):
        return (lax.rem(y, 2) * 4 + z, x * 4 + (y // 2) * 2 + c)

    def at(x=0, y=0, z=0, flip=False):
        return device(
            lax.rem(pos["x"] + x, 4), lax.rem(pos["y"] + y, 4), lax.rem(pos["z"] + z, 4),
            other if flip else core,
        )

    def send(src, dst, k, dev):
        pltpu.make_async_remote_copy(
            src, dst, ssem.at[k], rsem.at[k], device_id=dev, device_id_type=MESH
        ).start()

    me = at()

    def arrived(dst, k):
        pltpu.make_async_remote_copy(
            dst, dst, ssem.at[k], rsem.at[k], device_id=me, device_id_type=MESH
        ).wait_recv()

    def sent(src, k):
        pltpu.make_async_remote_copy(
            src, src, ssem.at[k], rsem.at[k], device_id=me, device_id_type=MESH
        ).wait_send()

    neighbours = [at(x=1), at(x=3), at(y=1), at(y=3), at(z=1), at(z=3)]
    x_up, x_down, y_two, mate = at(x=1), at(x=3), at(y=2), at(flip=True)

    home = 2 * y_lo + z // 2
    from_ylo = jnp.where(lax.rem(z, 2) == yh, y_lo, 1 - y_lo)
    from_z = lax.rem(z + pos["x"] - home + 7 - 2 * core, 4)
    near_dev = device(home, lax.rem(z, 2) * 2 + from_ylo, from_z, pos["x"] // 2)
    to_ylo = pos["x"] // 2
    to_z = 2 * lax.rem(pos["x"], 2) + yh
    to_yh = jnp.where(to_ylo == y_lo, yh, 1 - yh)
    to_x0 = lax.rem(pos["x"] + z - to_z + 5, 4)
    to_core = jnp.where(core == to_x0 // 2, 0, 1)
    to_x = lax.rem(to_x0 + 2 * to_core, 4)

    barrier = pltpu.get_barrier_semaphore()
    for dev in [*neighbours, y_two, mate, near_dev]:
        pl.semaphore_signal(barrier, inc=1, device_id=dev, device_id_type=MESH)

    def place(s):
        dx = jnp.where(s < 2, 2, jnp.where(s > 5, 0, 1 + 2 * lax.rem(s, 2)))
        same = jnp.where((s == 1) | (s == 4) | (s == 5) | (s == 7), 1, 0)
        return lax.rem(pos["x"] + dx, 4) * 2 + lax.rem(yh + 1 + same, 2)

    def load_a(s):
        return pltpu.make_async_copy(
            inv_ref.at[pl.ds(pl.multiple_of(place(s) * 256, 256), 256)], a.at[s], asem.at[s]
        )

    for s in range(2):
        load_a(s).start()
    small = [
        pltpu.make_async_copy(coup_ref, csp, lsem.at[2]),
        pltpu.make_async_copy(d1_ref, const.at[0], lsem.at[3]),
        pltpu.make_async_copy(d2_ref, const.at[2], lsem.at[4]),
    ]

    def member(rows_ref, first, count):
        ids = lax.broadcasted_iota(jnp.int32, (8, 64), 0) + first
        hits = (ids == rows_ref[...].reshape(1, 64)).astype(F32)
        return jnp.sum(hits, axis=1, keepdims=True)[:count]

    for copy in tiny:
        copy.wait()
    for p, rows_ref in enumerate((rows1_ref, rows2_ref)):
        keep = member(rows_ref, col * 8, 8)
        loads[p].wait()
        for j in range(8):
            rows = slice(j * BLK, (j + 1) * BLK)
            hi, lo = split(fac[p, rows, :] * keep[j : j + 1, :])
            xh[rows, p * W : (p + 1) * W] = hi
            xl[rows, p * W : (p + 1) * W] = lo

    for s in range(2, NSTEP):
        load_a(s).start()
    for copy in small:
        copy.start()

    pl.semaphore_wait(barrier, 9)
    block = lax.rem(to_x, 2) * 4 + to_yh * 2 + to_core
    served = pl.ds(pl.multiple_of(block * BLK, BLK), BLK)
    send(fac.at[:, served], near, NEAR, device(to_x, to_yh * 2 + to_ylo, to_z, to_core))

    def compute(s):
        load_a(s).wait()
        base = place(s) * 2
        parts = []
        for half in (other, core):
            r0 = pl.multiple_of(half * BLK, BLK)
            parts.append(
                jnp.concatenate(
                    [
                        a[s, pl.ds(r0, BLK), j * BLK : (j + 1) * BLK]
                        * pat_ref[j, base + half].astype(F32)
                        for j in range(8)
                    ],
                    axis=1,
                )
            )
        out = dot3(split(jnp.concatenate(parts, axis=0)), (xh[...], xl[...]))
        for p in range(2):
            give[s, p] = out[:BLK, p * W : (p + 1) * W]
            own[s, p] = out[BLK:, p * W : (p + 1) * W]

    lo_rows, hi_rows = pl.ds(0, XR), pl.ds(XR, YR)

    def fold(s):
        arrived(got.at[s], CORE + s)
        own[s] += got[s]

    def leg1(w, s):
        send(own.at[s, 0, lo_rows], l1.at[w, 0], LEG1 + 2 * w, x_up)
        send(own.at[s, 1, lo_rows], l1.at[w, 1], LEG1 + 2 * w + 1, x_down)

    def leg2_up(w, s):
        send(own.at[s, 1, lo_rows], r2.at[w, 0, 1], LEG2 + w, x_up)

    def leg2_down(w, s):
        send(own.at[s, 0, lo_rows], r2.at[w, 1, 0], LEG2 + w, x_down)

    def relay(w, up, down):
        for d, s, dev in ((0, up, x_up), (1, down, x_down)):
            arrived(l1.at[w, d], LEG1 + 2 * w + d)
            own[s, d, :XR] += l1[w, d]
            send(own.at[s, d, lo_rows], r2.at[w, d, d], LEG2 + w, dev)

    def give_y(dx, s):
        send(own.at[s, :, hi_rows], yf.at[dx], YF + dx, y_two)

    def fold_y(dx, s):
        arrived(yf.at[dx], YF + dx)
        own[s, :, XR:] += yf[dx]

    def hear(k):
        pl.semaphore_wait(round_sem.at[k], 6)

    def tell(k):
        for dev in neighbours:
            pl.semaphore_signal(round_sem.at[k], inc=1, device_id=dev, device_id_type=MESH)

    def after(t):
        if t == 0:
            leg1(0, 0)
            give_y(2, 0)
        elif t == 1:
            leg1(1, 1)
        elif t == 2:
            leg2_up(0, 2)
            give_y(1, 2)
            hear(0)
            tell(1)
        elif t == 3:
            leg2_down(0, 3)
            give_y(3, 3)
        elif t == 4:
            leg2_up(1, 4)
        elif t == 5:
            leg2_down(1, 5)
            hear(1)
            tell(2)
        elif t == 6:
            give_y(0, 6)
            relay(0, 2, 3)
            fold_y(2, 1)
            send(own.at[1, 0, hi_rows], yl1.at[0], YLEG1, x_up)
            send(own.at[1, 1, hi_rows], yl1.at[1], YLEG1 + 1, x_down)

    def step(s, carry):
        compute(s)

        send(give.at[s], got.at[s], CORE + s, mate)
        for t in range(NSTEP - 1):

            @pl.when(s == t + 1)
            def _(t=t):
                fold(t)
                after(t)

        return carry

    tell(0)
    lax.fori_loop(0, NSTEP, step, 0)
    fold(7)
    relay(1, 4, 5)

    arrived(r2.at[0], LEG2)
    own[6, :, :XR] += r2[0, 0] + r2[0, 1]
    send(own.at[6, :, lo_rows], ry, YLEG, y_two)

    def second_leg(d, dx, s, dev):
        fold_y(dx, s)
        send(own.at[s, 1 - d, hi_rows], yr2.at[d, 1 - d], YLEG2, dev)
        arrived(yl1.at[d], YLEG1 + d)
        own[s, d, XR:] += yl1[d]
        send(own.at[s, d, hi_rows], yr2.at[d, d], YLEG2, dev)

    second_leg(0, 1, 4, x_up)

    for copy in small:
        copy.wait()
    coup = csp[...]
    c_split, ct_split = split(coup), split(coup.T)
    d1c = dot3(split(const[0]), c_split)
    const[1] = -d1c
    const[2] += dot3(ct_split, split(d1c))

    second_leg(1, 3, 5, x_down)

    arrived(near, NEAR)
    own_id = row * 16 + col
    n1 = near[0] * member(rows1_ref, own_id, 1)
    n2 = near[1] * member(rows2_ref, own_id, 1)
    n1c = dot3(split(n1), c_split)
    for k, v in enumerate((n1, n2, n1c)):
        nt[0, k], nt[1, k] = split(v.T)
    nn[0], nn[1] = split(n2)

    fold_y(0, 7)
    arrived(r2.at[1], LEG2 + 1)
    own[7, :, :XR] += r2[1, 0] + r2[1, 1]
    arrived(yr2, YLEG2)
    own[7, :, XR:] += yr2[0] + yr2[1]
    hear(2)
    arrived(ry, YLEG)
    own[7, :, :XR] += ry[...]

    mine, theirs = pl.multiple_of(core * BLK, BLK), pl.multiple_of(other * BLK, BLK)
    half = pl.ds(mine, BLK)

    def put(m, value):
        g[m] = value
        send(g.at[m, pl.ds(theirs, BLK)], gc.at[m], GC + m, mate)

    m1, m2 = own[7, 0], own[7, 1]
    m1s, m1t = split(m1), split(m1.T)
    n1t, n2t, n1ct = ((nt[0, k], nt[1, k]) for k in range(3))
    n2s = (nn[0], nn[1])
    put(0, dot3(n1t, m1s))
    mc = dot3(m1s, c_split)
    mcs = split(mc)
    minus = lambda v: tuple(-u for u in v)
    put(1, dot3(join((m1t, n1t), 1), join((n2s, minus(mcs)), 0)))
    p2 = mc - m2
    put(2, dot3(join((n2t, split(mc.T), n1ct), 1), join((split(-p2), minus(n2s), mcs), 0)))
    p1_out[...] = -m1
    p2_out[...] = p2
    planes = (("x", "y", "z"), ("y", "z", "x"), ("z", "x", "y"))

    def shifted(m, i, j, k):
        return at(**dict(zip(planes[m], (i, j, k))))

    def piece(m, i, j):
        u, v, _ = planes[m]
        index = lax.rem(pos[u] + i, 4) * 4 + lax.rem(pos[v] + j, 4)
        return pl.ds(pl.multiple_of(mine + index * 8, 8), 8)

    order = sorted(
        ((i, j) for i in range(4) for j in range(4) if (i, j) != (0, 0)),
        key=lambda q: -(min(q[0], 4 - q[0]) + min(q[1], 4 - q[1])),
    )
    for m in range(3):
        arrived(gc.at[m], GC + m)
        g[m, half] += gc[m]
        for i, j in order:
            send(g.at[m, piece(m, i, j)], r1.at[m, i * 4 + j], R1 + m, shifted(m, i, j, 0))
    for m in range(3):
        arrived(r1.at[m, 1:16], R1 + m)
        total = g[m, piece(m, 0, 0)]
        for q in range(1, 16):
            total += r1[m, q]
        slot = pos[planes[m][2]]
        zs[m, slot] = total
        for k in (2, 1, 3):
            send(zs.at[m, slot], zs.at[m, slot], R2 + m, shifted(m, 0, 0, k))
    for m in range(3):
        arrived(zs.at[m, 1:4], R2 + m)
        at_piece = piece(m, 0, 0)
        res[m, at_piece] = const[m, at_piece] + ((zs[m, 0] + zs[m, 1]) + (zs[m, 2] + zs[m, 3]))
        for i, j in order:
            send(res.at[m, at_piece], res.at[m, at_piece], R3 + m, shifted(m, i, j, 0))
    for m in range(3):
        arrived(res.at[m, 0:120], R3 + m)
        send(res.at[m, half], res.at[m, half], GF + m, mate)
    for m, out in enumerate((b1_out, bc_out, b2_out)):
        arrived(res.at[m, pl.ds(theirs, BLK)], GF + m)
        out[...] = res[m]

    for s in range(NSTEP):
        sent(give.at[s], CORE + s)

    sent(near, NEAR)
    for k in range(4):
        sent(l1.at[0, 0], LEG1 + k)
        sent(yf.at[0], YF + k)
    for k in range(2):
        sent(r2.at[k], LEG2 + k)
        sent(yl1.at[0], YLEG1 + k)
    sent(ry, YLEG)
    sent(yr2, YLEG2)
    for m in range(3):
        sent(gc.at[m], GC + m)
        sent(r1.at[m, 1:16], R1 + m)
        sent(r1.at[m, 1:4], R2 + m)
        sent(r1.at[m, 1:16], R3 + m)
        sent(gc.at[m], GF + m)


def per_device(inverse, pattern, first, second, rows1, rows2, coupling, diag1, diag2):
    any_, vmem = pl.BlockSpec(memory_space=pl.ANY), pl.BlockSpec(memory_space=pltpu.VMEM)
    V = pltpu.VMEM
    outs = pl.pallas_call(
        kernel,
        out_shape=[V((BLK, W), F32)] * 2 + [V((W, W), F32)] * 3,
        in_specs=[pl.BlockSpec(memory_space=pltpu.HBM)] * 9,
        out_specs=[vmem] * 5,
        scratch_shapes=[
            V((8, 256, 1024), F32),
            V((2, 1024, W), F32),
            V((1024, 2 * W), BF16),
            V((1024, 2 * W), BF16),
            V((8, 2, BLK, W), F32),
            V((8, 2, BLK, W), F32),
            V((8, 2, BLK, W), F32),
            V((2, BLK, W), F32),
            V((2, 3, W, BLK), BF16),
            V((2, BLK, W), BF16),
            V((2, 2, XR, W), F32),
            V((2, 2, 2, XR, W), F32),
            V((2, XR, W), F32),
            V((4, 2, YR, W), F32),
            V((2, YR, W), F32),
            V((2, 2, YR, W), F32),
            V((3, W, W), F32),
            V((3, BLK, W), F32),
            V((3, 16, 8, W), F32),
            V((3, 4, 8, W), F32),
            V((3, W, W), F32),
            V((3, W, W), F32),
            V((W, W), F32),
            V((64,), jnp.int32),
            V((64,), jnp.int32),
            pltpu.SMEM((8, 16), jnp.int32),
            pltpu.SemaphoreType.DMA((NSEM,)),
            pltpu.SemaphoreType.DMA((NSEM,)),
            pltpu.SemaphoreType.DMA((8,)),
            pltpu.SemaphoreType.DMA((8,)),
            pltpu.SemaphoreType.REGULAR((ROUNDS,)),
        ],
        compiler_params=pltpu.CompilerParams(
            collective_id=0, has_side_effects=True, vmem_limit_bytes=60 * 2**20
        ),
    )(inverse, pattern.T, first, second, rows1, rows2, coupling, diag1, diag2)
    return pl.pallas_call(
        hand_over,
        out_shape=[jax.ShapeDtypeStruct(o.shape, o.dtype) for o in outs],
        in_specs=[vmem] * 5,
        out_specs=[any_] * 5,
        scratch_shapes=[pltpu.SemaphoreType.DMA((5,))],
    )(*[pltpu.with_memory_space_constraint(o, pltpu.VMEM) for o in outs])


def hand_over(*refs):
    sem = refs[-1]
    copies = [pltpu.make_async_copy(refs[i], refs[5 + i], sem.at[i]) for i in range(5)]
    for copy in copies:
        copy.start()
    for copy in copies:
        copy.wait()


def solution(mesh):
    return jax.shard_map(
        per_device,
        mesh=mesh,
        in_specs=(
            P("row", "col"), P("row", "col"), P("col", None), P("col", None),
            P(), P(), P(), P(), P(),
        ),
        out_specs=(P(("row", "col"), None), P(("row", "col"), None), P(), P(), P()),
        check_vma=False,
    )
```

```python
import functools

import jax
import jax.numpy as jnp
from jax import lax
from jax.experimental import pallas as pl
from jax.experimental.pallas import tpu as pltpu
from jax.sharding import PartitionSpec as P

MESH = pl.DeviceIdType.MESH
F32 = jnp.float32
BF16 = jnp.bfloat16
BLK = 128
W = 256
XR = 72
YR = BLK - XR
NSTEP = 8
SLOT = {"2o": 0, "2w": 1, "1o": 2, "3o": 3, "1w": 4, "3w": 5, "0o": 6, "0w": 7}

CORE = 0
NEAR = CORE + 8
LEG1 = NEAR + 1
LEG2 = LEG1 + 4
YLEG = LEG2 + 2
YF = YLEG + 1
YLEG1 = YF + 4
YLEG2 = YLEG1 + 2
GC = YLEG2 + 1
R1 = GC + 3
R2 = R1 + 3
R3 = R2 + 3
GF = R3 + 3
NSEM = GF + 3
ROUNDS = 3


def split(a):
    hi = a.astype(BF16)
    return hi, (a - hi.astype(F32)).astype(BF16)


def dot3(a, b):
    d = functools.partial(jnp.dot, preferred_element_type=F32)
    (ah, al), (bh, bl) = a, b
    return d(ah, bh) + d(al, bh) + d(ah, bl)


def join(parts, axis):
    return tuple(jnp.concatenate(p, axis=axis) for p in zip(*parts))


def kernel(
    inv_ref, pat_hbm, f1_ref, f2_ref, rows1_hbm, rows2_hbm, coup_ref, d1_ref, d2_ref,
    p1_out, p2_out, b1_out, bc_out, b2_out,
    a, fac, xh, xl, own, give, got, near, nt, nn, l1, r2, ry, yf, yl1, yr2,
    g, gc, r1, zs, res, const, csp, rows1_ref, rows2_ref, pat_ref,
    ssem, rsem, lsem, asem, round_sem,
):
    loads = [
        pltpu.make_async_copy(f1_ref, fac.at[0], lsem.at[0]),
        pltpu.make_async_copy(f2_ref, fac.at[1], lsem.at[1]),
    ]
    tiny = [
        pltpu.make_async_copy(rows1_hbm, rows1_ref, lsem.at[5]),
        pltpu.make_async_copy(rows2_hbm, rows2_ref, lsem.at[6]),
        pltpu.make_async_copy(pat_hbm, pat_ref, lsem.at[7]),
    ]
    for copy in tiny + loads:
        copy.start()

    row, col = lax.axis_index("row"), lax.axis_index("col")
    core = lax.rem(col, 2)
    y_lo, z, yh = row // 4, lax.rem(row, 4), lax.rem(col // 2, 2)
    pos = {"x": col // 4, "y": yh * 2 + y_lo, "z": z}
    other = 1 - core

    def device(x, y, z, c):
        return (lax.rem(y, 2) * 4 + z, x * 4 + (y // 2) * 2 + c)

    def at(x=0, y=0, z=0, flip=False):
        return device(
            lax.rem(pos["x"] + x, 4), lax.rem(pos["y"] + y, 4), lax.rem(pos["z"] + z, 4),
            other if flip else core,
        )

    def send(src, dst, k, dev, group=1):
        pltpu.make_async_remote_copy(
            src, dst, ssem.at[group], rsem.at[k], device_id=dev, device_id_type=MESH
        ).start()

    me = at()

    def arrived(dst, k):
        pltpu.make_async_remote_copy(
            dst, dst, ssem.at[0], rsem.at[k], device_id=me, device_id_type=MESH
        ).wait_recv()

    def sent(like, group):
        pltpu.make_async_remote_copy(
            like, like, ssem.at[group], rsem.at[0], device_id=me, device_id_type=MESH
        ).wait_send()

    neighbours = [at(x=1), at(x=3), at(y=1), at(y=3), at(z=1), at(z=3)]
    x_up, x_down, y_two, mate = at(x=1), at(x=3), at(y=2), at(flip=True)

    home = 2 * y_lo + z // 2
    from_ylo = jnp.where(lax.rem(z, 2) == yh, y_lo, 1 - y_lo)
    from_z = lax.rem(z + pos["x"] - home + 7 - 2 * core, 4)
    near_dev = device(home, lax.rem(z, 2) * 2 + from_ylo, from_z, pos["x"] // 2)
    to_ylo = pos["x"] // 2
    to_z = 2 * lax.rem(pos["x"], 2) + yh
    to_yh = jnp.where(to_ylo == y_lo, yh, 1 - yh)
    to_x0 = lax.rem(pos["x"] + z - to_z + 5, 4)
    to_core = jnp.where(core == to_x0 // 2, 0, 1)
    to_x = lax.rem(to_x0 + 2 * to_core, 4)

    barrier = pltpu.get_barrier_semaphore()
    for dev in [*neighbours, y_two, mate, near_dev]:
        pl.semaphore_signal(barrier, inc=1, device_id=dev, device_id_type=MESH)

    def place(s):
        dx = jnp.where(s < 2, 2, jnp.where(s > 5, 0, 1 + 2 * lax.rem(s, 2)))
        same = jnp.where((s == 1) | (s == 4) | (s == 5) | (s == 7), 1, 0)
        return lax.rem(pos["x"] + dx, 4) * 2 + lax.rem(yh + 1 + same, 2)

    def load_a(s):
        return pltpu.make_async_copy(
            inv_ref.at[pl.ds(pl.multiple_of(place(s) * 256, 256), 256)], a.at[s], asem.at[s]
        )

    for s in range(2):
        load_a(s).start()
    small = [
        pltpu.make_async_copy(coup_ref, csp, lsem.at[2]),
        pltpu.make_async_copy(d1_ref, const.at[0], lsem.at[3]),
        pltpu.make_async_copy(d2_ref, const.at[2], lsem.at[4]),
    ]

    def member(rows_ref, first, count):
        ids = lax.broadcasted_iota(jnp.int32, (8, 64), 0) + first
        hits = (ids == rows_ref[...].reshape(1, 64)).astype(F32)
        return jnp.sum(hits, axis=1, keepdims=True)[:count]

    for copy in tiny:
        copy.wait()
    for p, rows_ref in enumerate((rows1_ref, rows2_ref)):
        keep = member(rows_ref, col * 8, 8)
        loads[p].wait()
        for j in range(8):
            rows = slice(j * BLK, (j + 1) * BLK)
            hi, lo = split(fac[p, rows, :] * keep[j : j + 1, :])
            xh[rows, p * W : (p + 1) * W] = hi
            xl[rows, p * W : (p + 1) * W] = lo

    for s in range(2, NSTEP):
        load_a(s).start()
    for copy in small:
        copy.start()

    pl.semaphore_wait(barrier, 9)
    block = lax.rem(to_x, 2) * 4 + to_yh * 2 + to_core
    served = pl.ds(pl.multiple_of(block * BLK, BLK), BLK)
    send(fac.at[:, served], near, NEAR, device(to_x, to_yh * 2 + to_ylo, to_z, to_core))

    def compute(s):
        load_a(s).wait()
        base = place(s) * 2
        parts = []
        for half in (other, core):
            r0 = pl.multiple_of(half * BLK, BLK)
            parts.append(
                jnp.concatenate(
                    [
                        a[s, pl.ds(r0, BLK), j * BLK : (j + 1) * BLK]
                        * pat_ref[j, base + half].astype(F32)
                        for j in range(8)
                    ],
                    axis=1,
                )
            )
        out = dot3(split(jnp.concatenate(parts, axis=0)), (xh[...], xl[...]))
        for p in range(2):
            give[s, p] = out[:BLK, p * W : (p + 1) * W]
            own[s, p] = out[BLK:, p * W : (p + 1) * W]

    lo_rows, hi_rows = pl.ds(0, XR), pl.ds(XR, YR)

    def fold(s):
        arrived(got.at[s], CORE + s)
        own[s] += got[s]

    def leg1(w, s):
        send(own.at[s, 0, lo_rows], l1.at[w, 0], LEG1 + 2 * w, x_up)
        send(own.at[s, 1, lo_rows], l1.at[w, 1], LEG1 + 2 * w + 1, x_down)

    def leg2_up(w, s):
        send(own.at[s, 1, lo_rows], r2.at[w, 0, 1], LEG2 + w, x_up)

    def leg2_down(w, s):
        send(own.at[s, 0, lo_rows], r2.at[w, 1, 0], LEG2 + w, x_down)

    def relay(w, up, down):
        for d, s, dev in ((0, up, x_up), (1, down, x_down)):
            arrived(l1.at[w, d], LEG1 + 2 * w + d)
            own[s, d, :XR] += l1[w, d]
            send(own.at[s, d, lo_rows], r2.at[w, d, d], LEG2 + w, dev)

    def give_y(dx, s):
        send(own.at[s, :, hi_rows], yf.at[dx], YF + dx, y_two)

    def fold_y(dx, s):
        arrived(yf.at[dx], YF + dx)
        own[s, :, XR:] += yf[dx]

    def hear(k):
        pl.semaphore_wait(round_sem.at[k], 6)

    def tell(k):
        for dev in neighbours:
            pl.semaphore_signal(round_sem.at[k], inc=1, device_id=dev, device_id_type=MESH)

    def after(t):
        if t == 0:
            leg1(0, 0)
            give_y(2, 0)
        elif t == 1:
            leg1(1, 1)
        elif t == 2:
            leg2_up(0, 2)
            give_y(1, 2)
            hear(0)
            tell(1)
        elif t == 3:
            leg2_down(0, 3)
            give_y(3, 3)
        elif t == 4:
            leg2_up(1, 4)
            relay(0, 2, 3)
        elif t == 5:
            leg2_down(1, 5)
            hear(1)
            tell(2)
        elif t == 6:
            give_y(0, 6)
            fold_y(2, 1)
            send(own.at[1, 0, hi_rows], yl1.at[0], YLEG1, x_up)
            send(own.at[1, 1, hi_rows], yl1.at[1], YLEG1 + 1, x_down)
            relay(1, 4, 5)

    def step(s, carry):
        compute(s)

        send(give.at[s], got.at[s], CORE + s, mate, 0)
        for t in range(NSTEP - 1):

            @pl.when(s == t + 1)
            def _(t=t):
                fold(t)
                after(t)

        return carry

    tell(0)
    lax.fori_loop(0, NSTEP, step, 0)
    fold(7)

    fold_y(1, 4)
    send(own.at[4, 1, hi_rows], yr2.at[0, 1], YLEG2, x_up)

    arrived(r2.at[0], LEG2)
    own[6, :, :XR] += r2[0, 0] + r2[0, 1]
    send(own.at[6, :, lo_rows], ry, YLEG, y_two)

    fold_y(3, 5)
    send(own.at[5, 0, hi_rows], yr2.at[1, 0], YLEG2, x_down)
    for d, s, dev in ((0, 4, x_up), (1, 5, x_down)):
        arrived(yl1.at[d], YLEG1 + d)
        own[s, d, XR:] += yl1[d]
        send(own.at[s, d, hi_rows], yr2.at[d, d], YLEG2, dev)

    for copy in small:
        copy.wait()
    coup = csp[...]
    c_split, ct_split = split(coup), split(coup.T)
    d1c = dot3(split(const[0]), c_split)
    const[1] = -d1c
    const[2] += dot3(ct_split, split(d1c))

    arrived(near, NEAR)
    own_id = row * 16 + col
    n1 = near[0] * member(rows1_ref, own_id, 1)
    n2 = near[1] * member(rows2_ref, own_id, 1)
    n1c = dot3(split(n1), c_split)
    for k, v in enumerate((n1, n2, n1c)):
        nt[0, k], nt[1, k] = split(v.T)
    nn[0], nn[1] = split(n2)

    fold_y(0, 7)
    arrived(r2.at[1], LEG2 + 1)
    own[7, :, :XR] += r2[1, 0] + r2[1, 1]
    arrived(yr2, YLEG2)
    own[7, :, XR:] += yr2[0] + yr2[1]
    hear(2)
    arrived(ry, YLEG)
    own[7, :, :XR] += ry[...]

    mine, theirs = pl.multiple_of(core * BLK, BLK), pl.multiple_of(other * BLK, BLK)
    half = pl.ds(mine, BLK)

    def put(m, value):
        g[m] = value
        send(g.at[m, pl.ds(theirs, BLK)], gc.at[m], GC + m, mate)

    m1, m2 = own[7, 0], own[7, 1]
    m1s, m1t = split(m1), split(m1.T)
    n1t, n2t, n1ct = ((nt[0, k], nt[1, k]) for k in range(3))
    n2s = (nn[0], nn[1])
    put(0, dot3(n1t, m1s))
    mc = dot3(m1s, c_split)
    mcs = split(mc)
    minus = lambda v: tuple(-u for u in v)
    put(1, dot3(join((m1t, n1t), 1), join((n2s, minus(mcs)), 0)))
    p2 = mc - m2
    put(2, dot3(join((n2t, split(mc.T), n1ct), 1), join((split(-p2), minus(n2s), mcs), 0)))
    p1_out[...] = -m1
    p2_out[...] = p2
    planes = (("x", "y", "z"), ("y", "z", "x"), ("z", "x", "y"))

    def shifted(m, i, j, k):
        return at(**dict(zip(planes[m], (i, j, k))))

    def piece(m, i, j):
        u, v, _ = planes[m]
        index = lax.rem(pos[u] + i, 4) * 4 + lax.rem(pos[v] + j, 4)
        return pl.ds(pl.multiple_of(mine + index * 8, 8), 8)

    order = sorted(
        ((i, j) for i in range(4) for j in range(4) if (i, j) != (0, 0)),
        key=lambda q: -(min(q[0], 4 - q[0]) + min(q[1], 4 - q[1])),
    )
    for m in range(3):
        arrived(gc.at[m], GC + m)
        g[m, half] += gc[m]
        for i, j in order:
            send(g.at[m, piece(m, i, j)], r1.at[m, i * 4 + j], R1 + m, shifted(m, i, j, 0), 2)
    for m in range(3):
        arrived(r1.at[m, 1:16], R1 + m)
        total = g[m, piece(m, 0, 0)]
        for q in range(1, 16):
            total += r1[m, q]
        slot = pos[planes[m][2]]
        zs[m, slot] = total
        for k in (2, 1, 3):
            send(zs.at[m, slot], zs.at[m, slot], R2 + m, shifted(m, 0, 0, k), 2)
    for m in range(3):
        arrived(zs.at[m, 1:4], R2 + m)
        at_piece = piece(m, 0, 0)
        res[m, at_piece] = const[m, at_piece] + ((zs[m, 0] + zs[m, 1]) + (zs[m, 2] + zs[m, 3]))
        for i, j in order:
            send(res.at[m, at_piece], res.at[m, at_piece], R3 + m, shifted(m, i, j, 0), 2)
    for m in range(3):
        arrived(res.at[m, 0:120], R3 + m)
        send(res.at[m, half], res.at[m, half], GF + m, mate)
    for m, out in enumerate((b1_out, bc_out, b2_out)):
        arrived(res.at[m, pl.ds(theirs, BLK)], GF + m)
        out[...] = res[m]

    sent(give, 0)
    rows = 2 * BLK + 12 * XR + 2 * XR + 14 * YR + 6 * BLK
    sent(a.at[0:4, 0 : rows // 16], 1)
    sent(fac.at[0, 0 : 3 * (120 + 24 + 120)], 2)


def per_device(inverse, pattern, first, second, rows1, rows2, coupling, diag1, diag2):
    any_, vmem = pl.BlockSpec(memory_space=pl.ANY), pl.BlockSpec(memory_space=pltpu.VMEM)
    V = pltpu.VMEM
    outs = pl.pallas_call(
        kernel,
        out_shape=[V((BLK, W), F32)] * 2 + [V((W, W), F32)] * 3,
        in_specs=[pl.BlockSpec(memory_space=pltpu.HBM)] * 9,
        out_specs=[vmem] * 5,
        scratch_shapes=[
            V((8, 256, 1024), F32),
            V((2, 1024, W), F32),
            V((1024, 2 * W), BF16),
            V((1024, 2 * W), BF16),
            V((8, 2, BLK, W), F32),
            V((8, 2, BLK, W), F32),
            V((8, 2, BLK, W), F32),
            V((2, BLK, W), F32),
            V((2, 3, W, BLK), BF16),
            V((2, BLK, W), BF16),
            V((2, 2, XR, W), F32),
            V((2, 2, 2, XR, W), F32),
            V((2, XR, W), F32),
            V((4, 2, YR, W), F32),
            V((2, YR, W), F32),
            V((2, 2, YR, W), F32),
            V((3, W, W), F32),
            V((3, BLK, W), F32),
            V((3, 16, 8, W), F32),
            V((3, 4, 8, W), F32),
            V((3, W, W), F32),
            V((3, W, W), F32),
            V((W, W), F32),
            V((64,), jnp.int32),
            V((64,), jnp.int32),
            pltpu.SMEM((8, 16), jnp.int32),
            pltpu.SemaphoreType.DMA((3,)),
            pltpu.SemaphoreType.DMA((NSEM,)),
            pltpu.SemaphoreType.DMA((8,)),
            pltpu.SemaphoreType.DMA((8,)),
            pltpu.SemaphoreType.REGULAR((ROUNDS,)),
        ],
        compiler_params=pltpu.CompilerParams(
            collective_id=0, has_side_effects=True, vmem_limit_bytes=60 * 2**20
        ),
    )(inverse, pattern.T, first, second, rows1, rows2, coupling, diag1, diag2)
    return pl.pallas_call(
        hand_over,
        out_shape=[jax.ShapeDtypeStruct(o.shape, o.dtype) for o in outs],
        in_specs=[vmem] * 5,
        out_specs=[any_] * 5,
        scratch_shapes=[pltpu.SemaphoreType.DMA((5,))],
    )(*[pltpu.with_memory_space_constraint(o, pltpu.VMEM) for o in outs])


def hand_over(*refs):
    sem = refs[-1]
    copies = [pltpu.make_async_copy(refs[i], refs[5 + i], sem.at[i]) for i in range(5)]
    for copy in copies:
        copy.start()
    for copy in copies:
        copy.wait()


def solution(mesh):
    return jax.shard_map(
        per_device,
        mesh=mesh,
        in_specs=(
            P("row", "col"), P("row", "col"), P("col", None), P("col", None),
            P(), P(), P(), P(), P(),
        ),
        out_specs=(P(("row", "col"), None), P(("row", "col"), None), P(), P(), P()),
        check_vma=False,
    )
```

```python
import functools

import jax
import jax.numpy as jnp
from jax import lax
from jax.experimental import pallas as pl
from jax.experimental.pallas import tpu as pltpu
from jax.sharding import PartitionSpec as P

MESH = pl.DeviceIdType.MESH
F32 = jnp.float32
BF16 = jnp.bfloat16
BLK = 128
W = 256
XR = 72
YR = BLK - XR
NSTEP = 8
SLOT = {"2o": 0, "2w": 1, "1o": 2, "3o": 3, "1w": 4, "3w": 5, "0o": 6, "0w": 7}

CORE = 0
NEAR = CORE + 8
LEG1 = NEAR + 1
LEG2 = LEG1 + 4
YLEG = LEG2 + 2
YF = YLEG + 1
YLEG1 = YF + 4
YLEG2 = YLEG1 + 2
GC = YLEG2 + 1
R1 = GC + 3
R2 = R1 + 3
R3 = R2 + 3
GF = R3 + 3
NSEM = GF + 3
ROUNDS = 3


def split(a):
    hi = a.astype(BF16)
    return hi, (a - hi.astype(F32)).astype(BF16)


def dot3(a, b):
    d = functools.partial(jnp.dot, preferred_element_type=F32)
    (ah, al), (bh, bl) = a, b
    return d(ah, bh) + d(al, bh) + d(ah, bl)


def join(parts, axis):
    return tuple(jnp.concatenate(p, axis=axis) for p in zip(*parts))


def kernel(
    inv_ref, pat_hbm, f1_ref, f2_ref, rows1_hbm, rows2_hbm, coup_ref, d1_ref, d2_ref,
    p1_out, p2_out, b1_out, bc_out, b2_out,
    a, fac, xh, xl, own, give, got, near, nt, nn, l1, r2, ry, yf, yl1, yr2,
    g, gc, r1, zs, res, const, csp, rows1_ref, rows2_ref, pat_ref,
    ssem, rsem, lsem, asem, round_sem,
):
    loads = [
        pltpu.make_async_copy(f1_ref, fac.at[0], lsem.at[0]),
        pltpu.make_async_copy(f2_ref, fac.at[1], lsem.at[1]),
    ]
    tiny = [
        pltpu.make_async_copy(rows1_hbm, rows1_ref, lsem.at[5]),
        pltpu.make_async_copy(rows2_hbm, rows2_ref, lsem.at[6]),
        pltpu.make_async_copy(pat_hbm, pat_ref, lsem.at[7]),
    ]
    for copy in tiny + loads:
        copy.start()

    row, col = lax.axis_index("row"), lax.axis_index("col")
    core = lax.rem(col, 2)
    y_lo, z, yh = row // 4, lax.rem(row, 4), lax.rem(col // 2, 2)
    pos = {"x": col // 4, "y": yh * 2 + y_lo, "z": z}
    other = 1 - core

    def device(x, y, z, c):
        return (lax.rem(y, 2) * 4 + z, x * 4 + (y // 2) * 2 + c)

    def at(x=0, y=0, z=0, flip=False):
        return device(
            lax.rem(pos["x"] + x, 4), lax.rem(pos["y"] + y, 4), lax.rem(pos["z"] + z, 4),
            other if flip else core,
        )

    def send(src, dst, k, dev, group=1):
        pltpu.make_async_remote_copy(
            src, dst, ssem.at[group], rsem.at[k], device_id=dev, device_id_type=MESH
        ).start()

    me = at()

    def arrived(dst, k):
        pltpu.make_async_remote_copy(
            dst, dst, ssem.at[0], rsem.at[k], device_id=me, device_id_type=MESH
        ).wait_recv()

    def sent(like, group):
        pltpu.make_async_remote_copy(
            like, like, ssem.at[group], rsem.at[0], device_id=me, device_id_type=MESH
        ).wait_send()

    neighbours = [at(x=1), at(x=3), at(y=1), at(y=3), at(z=1), at(z=3)]
    x_up, x_down, y_two, mate = at(x=1), at(x=3), at(y=2), at(flip=True)

    home = 2 * y_lo + z // 2
    from_ylo = jnp.where(lax.rem(z, 2) == yh, y_lo, 1 - y_lo)
    from_z = lax.rem(z + pos["x"] - home + 7 - 2 * core, 4)
    near_dev = device(home, lax.rem(z, 2) * 2 + from_ylo, from_z, pos["x"] // 2)
    to_ylo = pos["x"] // 2
    to_z = 2 * lax.rem(pos["x"], 2) + yh
    to_yh = jnp.where(to_ylo == y_lo, yh, 1 - yh)
    to_x0 = lax.rem(pos["x"] + z - to_z + 5, 4)
    to_core = jnp.where(core == to_x0 // 2, 0, 1)
    to_x = lax.rem(to_x0 + 2 * to_core, 4)

    barrier = pltpu.get_barrier_semaphore()
    for dev in [near_dev, *neighbours, y_two, mate]:
        pl.semaphore_signal(barrier, inc=1, device_id=dev, device_id_type=MESH)

    def place(s):
        dx = jnp.where(s < 2, 2, jnp.where(s > 5, 0, 1 + 2 * lax.rem(s, 2)))
        same = jnp.where((s == 1) | (s == 4) | (s == 5) | (s == 7), 1, 0)
        return lax.rem(pos["x"] + dx, 4) * 2 + lax.rem(yh + 1 + same, 2)

    def load_a(s):
        return pltpu.make_async_copy(
            inv_ref.at[pl.ds(pl.multiple_of(place(s) * 256, 256), 256)], a.at[s], asem.at[s]
        )

    load_a(0).start()
    small = [
        pltpu.make_async_copy(coup_ref, csp, lsem.at[2]),
        pltpu.make_async_copy(d1_ref, const.at[0], lsem.at[3]),
        pltpu.make_async_copy(d2_ref, const.at[2], lsem.at[4]),
    ]

    def member(rows_ref, first, count):
        ids = lax.broadcasted_iota(jnp.int32, (8, 64), 0) + first
        hits = (ids == rows_ref[...].reshape(1, 64)).astype(F32)
        return jnp.sum(hits, axis=1, keepdims=True)[:count]

    for copy in tiny:
        copy.wait()
    for p, rows_ref in enumerate((rows1_ref, rows2_ref)):
        keep = member(rows_ref, col * 8, 8)
        loads[p].wait()
        for j in range(8):
            rows = slice(j * BLK, (j + 1) * BLK)
            hi, lo = split(fac[p, rows, :] * keep[j : j + 1, :])
            xh[rows, p * W : (p + 1) * W] = hi
            xl[rows, p * W : (p + 1) * W] = lo

    for s in range(1, NSTEP):
        load_a(s).start()
    for copy in small:
        copy.start()

    pl.semaphore_wait(barrier, 9)
    block = lax.rem(to_x, 2) * 4 + to_yh * 2 + to_core
    served = pl.ds(pl.multiple_of(block * BLK, BLK), BLK)
    send(fac.at[:, served], near, NEAR, device(to_x, to_yh * 2 + to_ylo, to_z, to_core))

    def compute(s):
        load_a(s).wait()
        base = place(s) * 2
        parts = []
        for half in (other, core):
            r0 = pl.multiple_of(half * BLK, BLK)
            parts.append(
                jnp.concatenate(
                    [
                        a[s, pl.ds(r0, BLK), j * BLK : (j + 1) * BLK]
                        * pat_ref[j, base + half].astype(F32)
                        for j in range(8)
                    ],
                    axis=1,
                )
            )
        out = dot3(split(jnp.concatenate(parts, axis=0)), (xh[...], xl[...]))
        for p in range(2):
            give[s, p] = out[:BLK, p * W : (p + 1) * W]
            own[s, p] = out[BLK:, p * W : (p + 1) * W]

    lo_rows, hi_rows = pl.ds(0, XR), pl.ds(XR, YR)

    def fold(s):
        arrived(got.at[s], CORE + s)
        own[s] += got[s]

    def leg1(w, s):
        send(own.at[s, 0, lo_rows], l1.at[w, 0], LEG1 + 2 * w, x_up)
        send(own.at[s, 1, lo_rows], l1.at[w, 1], LEG1 + 2 * w + 1, x_down)

    def leg2_up(w, s):
        send(own.at[s, 1, lo_rows], r2.at[w, 0, 1], LEG2 + w, x_up)

    def leg2_down(w, s):
        send(own.at[s, 0, lo_rows], r2.at[w, 1, 0], LEG2 + w, x_down)

    def relay(w, up, down):
        for d, s, dev in ((0, up, x_up), (1, down, x_down)):
            arrived(l1.at[w, d], LEG1 + 2 * w + d)
            own[s, d, :XR] += l1[w, d]
            send(own.at[s, d, lo_rows], r2.at[w, d, d], LEG2 + w, dev)

    def give_y(dx, s):
        send(own.at[s, :, hi_rows], yf.at[dx], YF + dx, y_two)

    def fold_y(dx, s):
        arrived(yf.at[dx], YF + dx)
        own[s, :, XR:] += yf[dx]

    def hear(k):
        pl.semaphore_wait(round_sem.at[k], 6)

    def tell(k):
        for dev in neighbours:
            pl.semaphore_signal(round_sem.at[k], inc=1, device_id=dev, device_id_type=MESH)

    def after(t):
        if t == 0:
            leg1(0, 0)
            give_y(2, 0)
        elif t == 1:
            leg1(1, 1)
        elif t == 2:
            leg2_up(0, 2)
            give_y(1, 2)
            hear(0)
            tell(1)
        elif t == 3:
            leg2_down(0, 3)
            give_y(3, 3)
        elif t == 4:
            leg2_up(1, 4)
            relay(0, 2, 3)
        elif t == 5:
            leg2_down(1, 5)
            hear(1)
            tell(2)
        elif t == 6:
            give_y(0, 6)
            fold_y(2, 1)
            send(own.at[1, 0, hi_rows], yl1.at[0], YLEG1, x_up)
            send(own.at[1, 1, hi_rows], yl1.at[1], YLEG1 + 1, x_down)
            relay(1, 4, 5)

    def step(s, carry):
        compute(s)

        send(give.at[s], got.at[s], CORE + s, mate, 0)
        for t in range(NSTEP - 1):

            @pl.when(s == t + 1)
            def _(t=t):
                fold(t)
                after(t)

        return carry

    tell(0)
    lax.fori_loop(0, NSTEP, step, 0)
    fold(7)

    fold_y(1, 4)
    send(own.at[4, 1, hi_rows], yr2.at[0, 1], YLEG2, x_up)

    arrived(r2.at[0], LEG2)
    own[6, :, :XR] += r2[0, 0] + r2[0, 1]
    send(own.at[6, :, lo_rows], ry, YLEG, y_two)

    fold_y(3, 5)
    send(own.at[5, 0, hi_rows], yr2.at[1, 0], YLEG2, x_down)
    for d, s, dev in ((0, 4, x_up), (1, 5, x_down)):
        arrived(yl1.at[d], YLEG1 + d)
        own[s, d, XR:] += yl1[d]
        send(own.at[s, d, hi_rows], yr2.at[d, d], YLEG2, dev)

    for copy in small:
        copy.wait()
    coup = csp[...]
    c_split, ct_split = split(coup), split(coup.T)
    d1c = dot3(split(const[0]), c_split)
    const[1] = -d1c
    const[2] += dot3(ct_split, split(d1c))

    arrived(near, NEAR)
    own_id = row * 16 + col
    n1 = near[0] * member(rows1_ref, own_id, 1)
    n2 = near[1] * member(rows2_ref, own_id, 1)
    n1c = dot3(split(n1), c_split)
    for k, v in enumerate((n1, n2, n1c)):
        nt[0, k], nt[1, k] = split(v.T)
    nn[0], nn[1] = split(n2)

    fold_y(0, 7)
    arrived(r2.at[1], LEG2 + 1)
    own[7, :, :XR] += r2[1, 0] + r2[1, 1]
    arrived(yr2, YLEG2)
    own[7, :, XR:] += yr2[0] + yr2[1]
    hear(2)
    arrived(ry, YLEG)
    own[7, :, :XR] += ry[...]

    mine, theirs = pl.multiple_of(core * BLK, BLK), pl.multiple_of(other * BLK, BLK)
    half = pl.ds(mine, BLK)

    def put(m, value):
        g[m] = value
        send(g.at[m, pl.ds(theirs, BLK)], gc.at[m], GC + m, mate)

    m1, m2 = own[7, 0], own[7, 1]
    m1s, m1t = split(m1), split(m1.T)
    n1t, n2t, n1ct = ((nt[0, k], nt[1, k]) for k in range(3))
    n2s = (nn[0], nn[1])
    put(0, dot3(n1t, m1s))
    mc = dot3(m1s, c_split)
    mcs = split(mc)
    minus = lambda v: tuple(-u for u in v)
    put(1, dot3(join((m1t, n1t), 1), join((n2s, minus(mcs)), 0)))
    p2 = mc - m2
    put(2, dot3(join((n2t, split(mc.T), n1ct), 1), join((split(-p2), minus(n2s), mcs), 0)))
    p1_out[...] = -m1
    p2_out[...] = p2
    planes = (("y", "z", "x"), ("z", "x", "y"), ("x", "y", "z"))

    def shifted(m, i, j, k):
        return at(**dict(zip(planes[m], (i, j, k))))

    def piece(m, i, j):
        u, v, _ = planes[m]
        index = lax.rem(pos[u] + i, 4) * 4 + lax.rem(pos[v] + j, 4)
        return pl.ds(pl.multiple_of(mine + index * 8, 8), 8)

    order = sorted(
        ((i, j) for i in range(4) for j in range(4) if (i, j) != (0, 0)),
        key=lambda q: -(min(q[0], 4 - q[0]) + min(q[1], 4 - q[1])),
    )
    for m in range(3):
        arrived(gc.at[m], GC + m)
        g[m, half] += gc[m]
        for i, j in order:
            send(g.at[m, piece(m, i, j)], r1.at[m, i * 4 + j], R1 + m, shifted(m, i, j, 0), 2)
    for m in range(3):
        arrived(r1.at[m, 1:16], R1 + m)
        total = g[m, piece(m, 0, 0)]
        for q in range(1, 16):
            total += r1[m, q]
        slot = pos[planes[m][2]]
        zs[m, slot] = total
        for k in (2, 1, 3):
            send(zs.at[m, slot], zs.at[m, slot], R2 + m, shifted(m, 0, 0, k), 2)
    for m in range(3):
        arrived(zs.at[m, 1:4], R2 + m)
        at_piece = piece(m, 0, 0)
        res[m, at_piece] = const[m, at_piece] + ((zs[m, 0] + zs[m, 1]) + (zs[m, 2] + zs[m, 3]))
        for i, j in order:
            send(res.at[m, at_piece], res.at[m, at_piece], R3 + m, shifted(m, i, j, 0), 2)
    for m in range(3):
        arrived(res.at[m, 0:120], R3 + m)
        send(res.at[m, half], res.at[m, half], GF + m, mate)
    for m, out in enumerate((b1_out, bc_out, b2_out)):
        arrived(res.at[m, pl.ds(theirs, BLK)], GF + m)
        out[...] = res[m]

    sent(give, 0)
    rows = 2 * BLK + 12 * XR + 2 * XR + 14 * YR + 6 * BLK
    sent(a.at[0:4, 0 : rows // 16], 1)
    sent(fac.at[0, 0 : 3 * (120 + 24 + 120)], 2)


def per_device(inverse, pattern, first, second, rows1, rows2, coupling, diag1, diag2):
    any_, vmem = pl.BlockSpec(memory_space=pl.ANY), pl.BlockSpec(memory_space=pltpu.VMEM)
    V = pltpu.VMEM
    outs = pl.pallas_call(
        kernel,
        out_shape=[V((BLK, W), F32)] * 2 + [V((W, W), F32)] * 3,
        in_specs=[pl.BlockSpec(memory_space=pltpu.HBM)] * 9,
        out_specs=[vmem] * 5,
        scratch_shapes=[
            V((8, 256, 1024), F32),
            V((2, 1024, W), F32),
            V((1024, 2 * W), BF16),
            V((1024, 2 * W), BF16),
            V((8, 2, BLK, W), F32),
            V((8, 2, BLK, W), F32),
            V((8, 2, BLK, W), F32),
            V((2, BLK, W), F32),
            V((2, 3, W, BLK), BF16),
            V((2, BLK, W), BF16),
            V((2, 2, XR, W), F32),
            V((2, 2, 2, XR, W), F32),
            V((2, XR, W), F32),
            V((4, 2, YR, W), F32),
            V((2, YR, W), F32),
            V((2, 2, YR, W), F32),
            V((3, W, W), F32),
            V((3, BLK, W), F32),
            V((3, 16, 8, W), F32),
            V((3, 4, 8, W), F32),
            V((3, W, W), F32),
            V((3, W, W), F32),
            V((W, W), F32),
            V((64,), jnp.int32),
            V((64,), jnp.int32),
            pltpu.SMEM((8, 16), jnp.int32),
            pltpu.SemaphoreType.DMA((3,)),
            pltpu.SemaphoreType.DMA((NSEM,)),
            pltpu.SemaphoreType.DMA((8,)),
            pltpu.SemaphoreType.DMA((8,)),
            pltpu.SemaphoreType.REGULAR((ROUNDS,)),
        ],
        compiler_params=pltpu.CompilerParams(
            collective_id=0, has_side_effects=True, vmem_limit_bytes=60 * 2**20
        ),
    )(inverse, pattern.T, first, second, rows1, rows2, coupling, diag1, diag2)
    return pl.pallas_call(
        hand_over,
        out_shape=[jax.ShapeDtypeStruct(o.shape, o.dtype) for o in outs],
        in_specs=[vmem] * 5,
        out_specs=[any_] * 5,
        scratch_shapes=[pltpu.SemaphoreType.DMA((5,))],
    )(*[pltpu.with_memory_space_constraint(o, pltpu.VMEM) for o in outs])


def hand_over(*refs):
    sem = refs[-1]
    copies = [pltpu.make_async_copy(refs[i], refs[5 + i], sem.at[i]) for i in range(5)]
    for copy in copies:
        copy.start()
    for copy in copies:
        copy.wait()


def solution(mesh):
    return jax.shard_map(
        per_device,
        mesh=mesh,
        in_specs=(
            P("row", "col"), P("row", "col"), P("col", None), P("col", None),
            P(), P(), P(), P(), P(),
        ),
        out_specs=(P(("row", "col"), None), P(("row", "col"), None), P(), P(), P()),
        check_vma=False,
    )
```

```python
import functools

import jax
import jax.numpy as jnp
from jax import lax
from jax.experimental import pallas as pl
from jax.experimental.pallas import tpu as pltpu
from jax.sharding import PartitionSpec as P

MESH = pl.DeviceIdType.MESH
F32 = jnp.float32
BF16 = jnp.bfloat16
BLK = 128
W = 256
XR = 72
YR = BLK - XR
NSTEP = 8
SLOT = {"2o": 0, "2w": 1, "1o": 2, "3o": 3, "1w": 4, "3w": 5, "0o": 6, "0w": 7}

CORE = 0
NEAR = CORE + 8
LEG1 = NEAR + 1
LEG2 = LEG1 + 4
YLEG = LEG2 + 2
YF = YLEG + 1
YLEG1 = YF + 4
YLEG2 = YLEG1 + 2
GC = YLEG2 + 1
R1 = GC + 3
R2 = R1 + 3
R3 = R2 + 3
GF = R3 + 3
NSEM = GF + 3
ROUNDS = 3


def split(a):
    hi = a.astype(BF16)
    return hi, (a - hi.astype(F32)).astype(BF16)


def dot3(a, b):
    d = functools.partial(jnp.dot, preferred_element_type=F32)
    (ah, al), (bh, bl) = a, b
    return d(ah, bh) + d(al, bh) + d(ah, bl)


def join(parts, axis):
    return tuple(jnp.concatenate(p, axis=axis) for p in zip(*parts))


def kernel(
    inv_ref, pat_hbm, f1_ref, f2_ref, rows1_hbm, rows2_hbm, coup_ref, d1_ref, d2_ref,
    p1_out, p2_out, b1_out, bc_out, b2_out,
    a, fac, xh, xl, own, give, got, near, nt, nn, l1, r2, ry, yf, yl1, yr2,
    g, gc, r1, zs, res, const, csp, rows1_ref, rows2_ref, pat_ref,
    ssem, rsem, lsem, asem, round_sem,
):
    loads = [
        pltpu.make_async_copy(f1_ref, fac.at[0], lsem.at[0]),
        pltpu.make_async_copy(f2_ref, fac.at[1], lsem.at[1]),
    ]
    tiny = [
        pltpu.make_async_copy(rows1_hbm, rows1_ref, lsem.at[3]),
        pltpu.make_async_copy(rows2_hbm, rows2_ref, lsem.at[4]),
        pltpu.make_async_copy(pat_hbm, pat_ref, lsem.at[5]),
    ]
    for copy in tiny + loads:
        copy.start()

    row, col = lax.axis_index("row"), lax.axis_index("col")
    core = lax.rem(col, 2)
    y_lo, z, yh = row // 4, lax.rem(row, 4), lax.rem(col // 2, 2)
    pos = {"x": col // 4, "y": yh * 2 + y_lo, "z": z}
    other = 1 - core

    def device(x, y, z, c):
        return (lax.rem(y, 2) * 4 + z, x * 4 + (y // 2) * 2 + c)

    def at(x=0, y=0, z=0, flip=False):
        return device(
            lax.rem(pos["x"] + x, 4), lax.rem(pos["y"] + y, 4), lax.rem(pos["z"] + z, 4),
            other if flip else core,
        )

    def send(src, dst, k, dev, group=1):
        pltpu.make_async_remote_copy(
            src, dst, ssem.at[group], rsem.at[k], device_id=dev, device_id_type=MESH
        ).start()

    me = at()

    def arrived(dst, k):
        pltpu.make_async_remote_copy(
            dst, dst, ssem.at[0], rsem.at[k], device_id=me, device_id_type=MESH
        ).wait_recv()

    def sent(like, group):
        pltpu.make_async_remote_copy(
            like, like, ssem.at[group], rsem.at[0], device_id=me, device_id_type=MESH
        ).wait_send()

    neighbours = [at(x=1), at(x=3), at(y=1), at(y=3), at(z=1), at(z=3)]
    x_up, x_down, y_two, mate = at(x=1), at(x=3), at(y=2), at(flip=True)

    home = 2 * y_lo + z // 2
    from_ylo = jnp.where(lax.rem(z, 2) == yh, y_lo, 1 - y_lo)
    from_z = lax.rem(z + pos["x"] - home + 7 - 2 * core, 4)
    near_dev = device(home, lax.rem(z, 2) * 2 + from_ylo, from_z, pos["x"] // 2)
    to_ylo = pos["x"] // 2
    to_z = 2 * lax.rem(pos["x"], 2) + yh
    to_yh = jnp.where(to_ylo == y_lo, yh, 1 - yh)
    to_x0 = lax.rem(pos["x"] + z - to_z + 5, 4)
    to_core = jnp.where(core == to_x0 // 2, 0, 1)
    to_x = lax.rem(to_x0 + 2 * to_core, 4)

    barrier = pltpu.get_barrier_semaphore()
    for dev in [near_dev, *neighbours, y_two, mate]:
        pl.semaphore_signal(barrier, inc=1, device_id=dev, device_id_type=MESH)

    def place(s):
        dx = jnp.where(s < 2, 2, jnp.where(s > 5, 0, 1 + 2 * lax.rem(s, 2)))
        same = jnp.where((s == 1) | (s == 4) | (s == 5) | (s == 7), 1, 0)
        return lax.rem(pos["x"] + dx, 4) * 2 + lax.rem(yh + 1 + same, 2)

    def load_a(s):
        return pltpu.make_async_copy(
            inv_ref.at[pl.ds(pl.multiple_of(place(s) * 256, 256), 256)], a.at[s], asem.at[s]
        )

    load_a(0).start()
    small = [
        pltpu.make_async_copy(coup_ref, csp, lsem.at[2]),
        pltpu.make_async_copy(d1_ref, const.at[0], lsem.at[2]),
        pltpu.make_async_copy(d2_ref, const.at[2], lsem.at[2]),
    ]

    def member(rows_ref, first, count):
        ids = lax.broadcasted_iota(jnp.int32, (8, 64), 0) + first
        hits = (ids == rows_ref[...].reshape(1, 64)).astype(F32)
        return jnp.sum(hits, axis=1, keepdims=True)[:count]

    for copy in tiny:
        copy.wait()
    for p, rows_ref in enumerate((rows1_ref, rows2_ref)):
        keep = member(rows_ref, col * 8, 8)
        loads[p].wait()
        for j in range(8):
            rows = slice(j * BLK, (j + 1) * BLK)
            hi, lo = split(fac[p, rows, :] * keep[j : j + 1, :])
            xh[rows, p * W : (p + 1) * W] = hi
            xl[rows, p * W : (p + 1) * W] = lo

    for s in range(1, NSTEP):
        load_a(s).start()
    for copy in small:
        copy.start()

    pl.semaphore_wait(barrier, 9)
    block = lax.rem(to_x, 2) * 4 + to_yh * 2 + to_core
    served = pl.ds(pl.multiple_of(block * BLK, BLK), BLK)
    send(fac.at[:, served], near, NEAR, device(to_x, to_yh * 2 + to_ylo, to_z, to_core))

    def compute(s):
        load_a(s).wait()
        base = place(s) * 2
        parts = []
        for half in (other, core):
            r0 = pl.multiple_of(half * BLK, BLK)
            parts.append(
                jnp.concatenate(
                    [
                        a[s, pl.ds(r0, BLK), j * BLK : (j + 1) * BLK]
                        * pat_ref[j, base + half].astype(F32)
                        for j in range(8)
                    ],
                    axis=1,
                )
            )
        out = dot3(split(jnp.concatenate(parts, axis=0)), (xh[...], xl[...]))
        for p in range(2):
            give[s, p] = out[:BLK, p * W : (p + 1) * W]
            own[s, p] = out[BLK:, p * W : (p + 1) * W]

    lo_rows, hi_rows = pl.ds(0, XR), pl.ds(XR, YR)

    def fold(s):
        arrived(got.at[s], CORE + s)
        own[s] += got[s]

    def leg1(w, s):
        send(own.at[s, 0, lo_rows], l1.at[w, 0], LEG1 + 2 * w, x_up)
        send(own.at[s, 1, lo_rows], l1.at[w, 1], LEG1 + 2 * w + 1, x_down)

    def leg2_up(w, s):
        send(own.at[s, 1, lo_rows], r2.at[w, 0, 1], LEG2 + w, x_up)

    def leg2_down(w, s):
        send(own.at[s, 0, lo_rows], r2.at[w, 1, 0], LEG2 + w, x_down)

    def relay(w, up, down):
        for d, s, dev in ((0, up, x_up), (1, down, x_down)):
            arrived(l1.at[w, d], LEG1 + 2 * w + d)
            own[s, d, :XR] += l1[w, d]
            send(own.at[s, d, lo_rows], r2.at[w, d, d], LEG2 + w, dev)

    def give_y(dx, s):
        send(own.at[s, :, hi_rows], yf.at[dx], YF + dx, y_two)

    def fold_y(dx, s):
        arrived(yf.at[dx], YF + dx)
        own[s, :, XR:] += yf[dx]

    def hear(k):
        pl.semaphore_wait(round_sem.at[k], 6)

    def tell(k):
        for dev in neighbours:
            pl.semaphore_signal(round_sem.at[k], inc=1, device_id=dev, device_id_type=MESH)

    def after(t):
        if t == 0:
            leg1(0, 0)
            give_y(2, 0)
        elif t == 1:
            leg1(1, 1)
        elif t == 2:
            leg2_up(0, 2)
            give_y(1, 2)
            hear(0)
            tell(1)
        elif t == 3:
            leg2_down(0, 3)
            give_y(3, 3)
        elif t == 4:
            leg2_up(1, 4)
            relay(0, 2, 3)
        elif t == 5:
            leg2_down(1, 5)
            hear(1)
            tell(2)
        elif t == 6:
            give_y(0, 6)
            fold_y(2, 1)
            send(own.at[1, 0, hi_rows], yl1.at[0], YLEG1, x_up)
            send(own.at[1, 1, hi_rows], yl1.at[1], YLEG1 + 1, x_down)
            relay(1, 4, 5)

    def step(s, carry):
        compute(s)

        send(give.at[s], got.at[s], CORE + s, mate, 0)
        for t in range(NSTEP - 1):

            @pl.when(s == t + 1)
            def _(t=t):
                fold(t)
                after(t)

        return carry

    tell(0)
    lax.fori_loop(0, NSTEP, step, 0)
    fold(7)

    fold_y(1, 4)
    send(own.at[4, 1, hi_rows], yr2.at[0, 1], YLEG2, x_up)

    arrived(r2.at[0], LEG2)
    own[6, :, :XR] += r2[0, 0] + r2[0, 1]
    send(own.at[6, :, lo_rows], ry, YLEG, y_two)

    fold_y(3, 5)
    send(own.at[5, 0, hi_rows], yr2.at[1, 0], YLEG2, x_down)
    for d, s, dev in ((0, 4, x_up), (1, 5, x_down)):
        arrived(yl1.at[d], YLEG1 + d)
        own[s, d, XR:] += yl1[d]
        send(own.at[s, d, hi_rows], yr2.at[d, d], YLEG2, dev)

    pltpu.make_async_copy(const, const, lsem.at[2]).wait()
    coup = csp[...]
    c_split, ct_split = split(coup), split(coup.T)
    d1c = dot3(split(const[0]), c_split)
    const[1] = -d1c
    const[2] += dot3(ct_split, split(d1c))

    arrived(near, NEAR)
    own_id = row * 16 + col
    n1 = near[0] * member(rows1_ref, own_id, 1)
    n2 = near[1] * member(rows2_ref, own_id, 1)
    n1c = dot3(split(n1), c_split)
    for k, v in enumerate((n1, n2, n1c)):
        nt[0, k], nt[1, k] = split(v.T)
    nn[0], nn[1] = split(n2)

    fold_y(0, 7)
    arrived(r2.at[1], LEG2 + 1)
    own[7, :, :XR] += r2[1, 0] + r2[1, 1]
    arrived(yr2, YLEG2)
    own[7, :, XR:] += yr2[0] + yr2[1]
    hear(2)
    arrived(ry, YLEG)
    own[7, :, :XR] += ry[...]

    mine, theirs = pl.multiple_of(core * BLK, BLK), pl.multiple_of(other * BLK, BLK)
    half = pl.ds(mine, BLK)

    def put(m, value):
        g[m] = value
        send(g.at[m, pl.ds(theirs, BLK)], gc.at[m], GC + m, mate)

    m1, m2 = own[7, 0], own[7, 1]
    m1s, m1t = split(m1), split(m1.T)
    n1t, n2t, n1ct = ((nt[0, k], nt[1, k]) for k in range(3))
    n2s = (nn[0], nn[1])
    put(0, dot3(n1t, m1s))
    mc = dot3(m1s, c_split)
    mcs = split(mc)
    minus = lambda v: tuple(-u for u in v)
    put(1, dot3(join((m1t, n1t), 1), join((n2s, minus(mcs)), 0)))
    p2 = mc - m2
    put(2, dot3(join((n2t, split(mc.T), n1ct), 1), join((split(-p2), minus(n2s), mcs), 0)))
    p1_out[...] = -m1
    p2_out[...] = p2
    planes = (("y", "z", "x"), ("z", "x", "y"), ("x", "y", "z"))

    def shifted(m, i, j, k):
        return at(**dict(zip(planes[m], (i, j, k))))

    def piece(m, i, j):
        u, v, _ = planes[m]
        index = lax.rem(pos[u] + i, 4) * 4 + lax.rem(pos[v] + j, 4)
        return pl.ds(pl.multiple_of(mine + index * 8, 8), 8)

    order = sorted(
        ((i, j) for i in range(4) for j in range(4) if (i, j) != (0, 0)),
        key=lambda q: -(1.01 * min(q[0], 4 - q[0]) + min(q[1], 4 - q[1])),
    )
    for m in range(3):
        arrived(gc.at[m], GC + m)
        g[m, half] += gc[m]
        for i, j in order:
            send(g.at[m, piece(m, i, j)], r1.at[m, i * 4 + j], R1 + m, shifted(m, i, j, 0), 2)
    for m in range(3):
        arrived(r1.at[m, 1:16], R1 + m)
        total = g[m, piece(m, 0, 0)]
        for q in range(1, 16):
            total += r1[m, q]
        slot = pos[planes[m][2]]
        zs[m, slot] = total
        for k in (2, 1, 3):
            send(zs.at[m, slot], zs.at[m, slot], R2 + m, shifted(m, 0, 0, k), 2)
    for m in range(3):
        arrived(zs.at[m, 1:4], R2 + m)
        at_piece = piece(m, 0, 0)
        res[m, at_piece] = const[m, at_piece] + ((zs[m, 0] + zs[m, 1]) + (zs[m, 2] + zs[m, 3]))
        for i, j in order:
            send(res.at[m, at_piece], res.at[m, at_piece], R3 + m, shifted(m, i, j, 0), 2)
    for m in range(3):
        arrived(res.at[m, 0:120], R3 + m)
        send(res.at[m, half], res.at[m, half], GF + m, mate)
    for m, out in enumerate((b1_out, bc_out, b2_out)):
        arrived(res.at[m, pl.ds(theirs, BLK)], GF + m)
        out[...] = res[m]

    sent(give, 0)
    rows = 2 * BLK + 12 * XR + 2 * XR + 14 * YR + 6 * BLK
    sent(a.at[0:4, 0 : rows // 16], 1)
    sent(fac.at[0, 0 : 3 * (120 + 24 + 120)], 2)


def per_device(inverse, pattern, first, second, rows1, rows2, coupling, diag1, diag2):
    any_, vmem = pl.BlockSpec(memory_space=pl.ANY), pl.BlockSpec(memory_space=pltpu.VMEM)
    V = pltpu.VMEM
    outs = pl.pallas_call(
        kernel,
        out_shape=[V((BLK, W), F32)] * 2 + [V((W, W), F32)] * 3,
        in_specs=[pl.BlockSpec(memory_space=pltpu.HBM)] * 9,
        out_specs=[vmem] * 5,
        scratch_shapes=[
            V((8, 256, 1024), F32),
            V((2, 1024, W), F32),
            V((1024, 2 * W), BF16),
            V((1024, 2 * W), BF16),
            V((8, 2, BLK, W), F32),
            V((8, 2, BLK, W), F32),
            V((8, 2, BLK, W), F32),
            V((2, BLK, W), F32),
            V((2, 3, W, BLK), BF16),
            V((2, BLK, W), BF16),
            V((2, 2, XR, W), F32),
            V((2, 2, 2, XR, W), F32),
            V((2, XR, W), F32),
            V((4, 2, YR, W), F32),
            V((2, YR, W), F32),
            V((2, 2, YR, W), F32),
            V((3, W, W), F32),
            V((3, BLK, W), F32),
            V((3, 16, 8, W), F32),
            V((3, 4, 8, W), F32),
            V((3, W, W), F32),
            V((3, W, W), F32),
            V((W, W), F32),
            V((64,), jnp.int32),
            V((64,), jnp.int32),
            pltpu.SMEM((8, 16), jnp.int32),
            pltpu.SemaphoreType.DMA((3,)),
            pltpu.SemaphoreType.DMA((NSEM,)),
            pltpu.SemaphoreType.DMA((6,)),
            pltpu.SemaphoreType.DMA((8,)),
            pltpu.SemaphoreType.REGULAR((ROUNDS,)),
        ],
        compiler_params=pltpu.CompilerParams(
            collective_id=0, has_side_effects=True, vmem_limit_bytes=60 * 2**20
        ),
    )(inverse, pattern.T, first, second, rows1, rows2, coupling, diag1, diag2)
    return pl.pallas_call(
        hand_over,
        out_shape=[jax.ShapeDtypeStruct(o.shape, o.dtype) for o in outs],
        in_specs=[vmem] * 5,
        out_specs=[any_] * 5,
        scratch_shapes=[pltpu.SemaphoreType.DMA((5,))],
    )(*[pltpu.with_memory_space_constraint(o, pltpu.VMEM) for o in outs])


def hand_over(*refs):
    sem = refs[-1]
    copies = [pltpu.make_async_copy(refs[i], refs[5 + i], sem.at[i]) for i in range(5)]
    for copy in copies:
        copy.start()
    for copy in copies:
        copy.wait()


def solution(mesh):
    return jax.shard_map(
        per_device,
        mesh=mesh,
        in_specs=(
            P("row", "col"), P("row", "col"), P("col", None), P("col", None),
            P(), P(), P(), P(), P(),
        ),
        out_specs=(P(("row", "col"), None), P(("row", "col"), None), P(), P(), P()),
        check_vma=False,
    )
```

```python
import functools

import jax
import jax.numpy as jnp
from jax import lax
from jax.experimental import pallas as pl
from jax.experimental.pallas import tpu as pltpu
from jax.sharding import PartitionSpec as P

MESH = pl.DeviceIdType.MESH
F32 = jnp.float32
BF16 = jnp.bfloat16
BLK = 128
W = 256
XR = 72
YR = BLK - XR
NSTEP = 8
SLOT = {"2o": 0, "2w": 1, "1o": 2, "3o": 3, "1w": 4, "3w": 5, "0o": 6, "0w": 7}

CORE = 0
NEAR = CORE + 8
LEG1 = NEAR + 1
LEG2 = LEG1 + 4
YLEG = LEG2 + 2
YF = YLEG + 1
YLEG1 = YF + 4
YLEG2 = YLEG1 + 2
GC = YLEG2 + 1
R1 = GC + 3
R2 = R1 + 3
R3 = R2 + 3
GF = R3 + 3
NSEM = GF + 3
ROUNDS = 3


def split(a):
    hi = a.astype(BF16)
    return hi, (a - hi.astype(F32)).astype(BF16)


def dot3(a, b):
    d = functools.partial(jnp.dot, preferred_element_type=F32)
    (ah, al), (bh, bl) = a, b
    return d(ah, bh) + d(al, bh) + d(ah, bl)


def join(parts, axis):
    return tuple(jnp.concatenate(p, axis=axis) for p in zip(*parts))


def kernel(
    inv_ref, pat_hbm, f1_ref, f2_ref, rows1_hbm, rows2_hbm, coup_ref, d1_ref, d2_ref,
    p1_out, p2_out, b1_out, bc_out, b2_out,
    a, fac, xh, xl, own, give, got, near, nt, nn, l1, r2, ry, yf, yl1, yr2,
    g, gc, r1, zs, res, const, csp, rows1_ref, rows2_ref, pat_ref,
    ssem, rsem, lsem, asem, round_sem,
):
    loads = [
        pltpu.make_async_copy(f1_ref, fac.at[0], lsem.at[0]),
        pltpu.make_async_copy(f2_ref, fac.at[1], lsem.at[1]),
    ]
    tiny = [
        pltpu.make_async_copy(rows1_hbm, rows1_ref, lsem.at[3]),
        pltpu.make_async_copy(rows2_hbm, rows2_ref, lsem.at[4]),
        pltpu.make_async_copy(pat_hbm, pat_ref, lsem.at[5]),
    ]
    for copy in tiny + loads:
        copy.start()

    row, col = lax.axis_index("row"), lax.axis_index("col")
    core = lax.rem(col, 2)
    y_lo, z, yh = row // 4, lax.rem(row, 4), lax.rem(col // 2, 2)
    pos = {"x": col // 4, "y": yh * 2 + y_lo, "z": z}
    other = 1 - core

    def device(x, y, z, c):
        return (lax.rem(y, 2) * 4 + z, x * 4 + (y // 2) * 2 + c)

    def at(x=0, y=0, z=0, flip=False):
        return device(
            lax.rem(pos["x"] + x, 4), lax.rem(pos["y"] + y, 4), lax.rem(pos["z"] + z, 4),
            other if flip else core,
        )

    def send(src, dst, k, dev, group=1):
        pltpu.make_async_remote_copy(
            src, dst, ssem.at[group], rsem.at[k], device_id=dev, device_id_type=MESH
        ).start()

    me = at()

    def arrived(dst, k):
        pltpu.make_async_remote_copy(
            dst, dst, ssem.at[0], rsem.at[k], device_id=me, device_id_type=MESH
        ).wait_recv()

    def sent(like, group):
        pltpu.make_async_remote_copy(
            like, like, ssem.at[group], rsem.at[0], device_id=me, device_id_type=MESH
        ).wait_send()

    neighbours = [at(x=1), at(x=3), at(y=1), at(y=3), at(z=1), at(z=3)]
    x_up, x_down, y_two, mate = at(x=1), at(x=3), at(y=2), at(flip=True)

    home = 2 * y_lo + z // 2
    from_ylo = jnp.where(lax.rem(z, 2) == yh, y_lo, 1 - y_lo)
    from_z = lax.rem(z + pos["x"] - home + 7 - 2 * core, 4)
    near_dev = device(home, lax.rem(z, 2) * 2 + from_ylo, from_z, pos["x"] // 2)
    to_ylo = pos["x"] // 2
    to_z = 2 * lax.rem(pos["x"], 2) + yh
    to_yh = jnp.where(to_ylo == y_lo, yh, 1 - yh)
    to_x0 = lax.rem(pos["x"] + z - to_z + 5, 4)
    to_core = jnp.where(core == to_x0 // 2, 0, 1)
    to_x = lax.rem(to_x0 + 2 * to_core, 4)

    barrier = pltpu.get_barrier_semaphore()
    for dev in [near_dev, *neighbours, y_two, mate]:
        pl.semaphore_signal(barrier, inc=1, device_id=dev, device_id_type=MESH)

    def place(s):
        dx = jnp.where(s < 2, 2, jnp.where(s > 5, 0, 1 + 2 * lax.rem(s, 2)))
        same = jnp.where((s == 1) | (s == 4) | (s == 5) | (s == 7), 1, 0)
        return lax.rem(pos["x"] + dx, 4) * 2 + lax.rem(yh + 1 + same, 2)

    def load_a(s):
        return pltpu.make_async_copy(
            inv_ref.at[pl.ds(pl.multiple_of(place(s) * 256, 256), 256)], a.at[s], asem.at[s]
        )

    load_a(0).start()
    small = [
        pltpu.make_async_copy(coup_ref, csp, lsem.at[2]),
        pltpu.make_async_copy(d1_ref, const.at[0], lsem.at[2]),
        pltpu.make_async_copy(d2_ref, const.at[2], lsem.at[2]),
    ]

    def member(rows_ref, first, count):
        ids = lax.broadcasted_iota(jnp.int32, (8, 64), 0) + first
        hits = (ids == rows_ref[...].reshape(1, 64)).astype(F32)
        return jnp.sum(hits, axis=1, keepdims=True)[:count]

    for copy in tiny:
        copy.wait()
    for p, rows_ref in enumerate((rows1_ref, rows2_ref)):
        keep = member(rows_ref, col * 8, 8)
        loads[p].wait()
        for j in range(8):
            rows = slice(j * BLK, (j + 1) * BLK)
            hi, lo = split(fac[p, rows, :] * keep[j : j + 1, :])
            xh[rows, p * W : (p + 1) * W] = hi
            xl[rows, p * W : (p + 1) * W] = lo

    for s in range(1, NSTEP):
        load_a(s).start()
    for copy in small:
        copy.start()

    pl.semaphore_wait(barrier, 9)
    block = lax.rem(to_x, 2) * 4 + to_yh * 2 + to_core
    served = pl.ds(pl.multiple_of(block * BLK, BLK), BLK)
    send(fac.at[:, served], near, NEAR, device(to_x, to_yh * 2 + to_ylo, to_z, to_core))

    def compute(s):
        load_a(s).wait()
        base = place(s) * 2
        parts = []
        for half in (other, core):
            r0 = pl.multiple_of(half * BLK, BLK)
            parts.append(
                jnp.concatenate(
                    [
                        a[s, pl.ds(r0, BLK), j * BLK : (j + 1) * BLK]
                        * pat_ref[j, base + half].astype(F32)
                        for j in range(8)
                    ],
                    axis=1,
                )
            )
        out = dot3(split(jnp.concatenate(parts, axis=0)), (xh[...], xl[...]))
        for p in range(2):
            give[s, p] = out[:BLK, p * W : (p + 1) * W]
            own[s, p] = out[BLK:, p * W : (p + 1) * W]

    lo_rows, hi_rows = pl.ds(0, XR), pl.ds(XR, YR)

    def fold(s):
        arrived(got.at[s], CORE + s)
        own[s] += got[s]

    def leg1(w, s):
        send(own.at[s, 0, lo_rows], l1.at[w, 0], LEG1 + 2 * w, x_up)
        send(own.at[s, 1, lo_rows], l1.at[w, 1], LEG1 + 2 * w + 1, x_down)

    def leg2_up(w, s):
        send(own.at[s, 1, lo_rows], r2.at[w, 0, 1], LEG2 + w, x_up)

    def leg2_down(w, s):
        send(own.at[s, 0, lo_rows], r2.at[w, 1, 0], LEG2 + w, x_down)

    def relay(w, up, down):
        for d, s, dev in ((0, up, x_up), (1, down, x_down)):
            arrived(l1.at[w, d], LEG1 + 2 * w + d)
            own[s, d, :XR] += l1[w, d]
            send(own.at[s, d, lo_rows], r2.at[w, d, d], LEG2 + w, dev)

    def give_y(dx, s):
        send(own.at[s, :, hi_rows], yf.at[dx], YF + dx, y_two)

    def fold_y(dx, s):
        arrived(yf.at[dx], YF + dx)
        own[s, :, XR:] += yf[dx]

    def hear(k):
        pl.semaphore_wait(round_sem.at[k], 6)

    def tell(k):
        for dev in neighbours:
            pl.semaphore_signal(round_sem.at[k], inc=1, device_id=dev, device_id_type=MESH)

    def after(t):
        if t == 0:
            leg1(0, 0)
            give_y(2, 0)
        elif t == 1:
            leg1(1, 1)
        elif t == 2:
            leg2_up(0, 2)
            give_y(1, 2)
            hear(0)
            tell(1)
        elif t == 3:
            leg2_down(0, 3)
            give_y(3, 3)
        elif t == 4:
            leg2_up(1, 4)
            relay(0, 2, 3)
        elif t == 5:
            leg2_down(1, 5)
            hear(1)
            tell(2)
        elif t == 6:
            give_y(0, 6)
            fold_y(2, 1)
            send(own.at[1, 0, hi_rows], yl1.at[0], YLEG1, x_up)
            send(own.at[1, 1, hi_rows], yl1.at[1], YLEG1 + 1, x_down)
            relay(1, 4, 5)

    def step(s, carry):
        compute(s)

        send(give.at[s], got.at[s], CORE + s, mate, 0)
        for t in range(NSTEP - 1):

            @pl.when(s == t + 1)
            def _(t=t):
                fold(t)
                after(t)

        return carry

    tell(0)
    lax.fori_loop(0, NSTEP, step, 0)
    fold(7)

    fold_y(1, 4)
    send(own.at[4, 1, hi_rows], yr2.at[0, 1], YLEG2, x_up)

    arrived(r2.at[0], LEG2)
    own[6, :, :XR] += r2[0, 0] + r2[0, 1]
    send(own.at[6, :, lo_rows], ry, YLEG, y_two)

    fold_y(3, 5)
    send(own.at[5, 0, hi_rows], yr2.at[1, 0], YLEG2, x_down)
    for d, s, dev in ((0, 4, x_up), (1, 5, x_down)):
        arrived(yl1.at[d], YLEG1 + d)
        own[s, d, XR:] += yl1[d]
        send(own.at[s, d, hi_rows], yr2.at[d, d], YLEG2, dev)

    pltpu.make_async_copy(const, const, lsem.at[2]).wait()
    coup = csp[...]
    c_split, ct_split = split(coup), split(coup.T)
    d1c = dot3(split(const[0]), c_split)
    const[1] = -d1c
    const[2] += dot3(ct_split, split(d1c))

    arrived(near, NEAR)
    own_id = row * 16 + col
    n1 = near[0] * member(rows1_ref, own_id, 1)
    n2 = near[1] * member(rows2_ref, own_id, 1)
    n1c = dot3(split(n1), c_split)
    for k, v in enumerate((n1, n2, n1c)):
        nt[0, k], nt[1, k] = split(v.T)
    nn[0], nn[1] = split(n2)

    fold_y(0, 7)
    arrived(r2.at[1], LEG2 + 1)
    own[7, :, :XR] += r2[1, 0] + r2[1, 1]
    arrived(yr2, YLEG2)
    own[7, :, XR:] += yr2[0] + yr2[1]
    hear(2)
    arrived(ry, YLEG)
    own[7, :, :XR] += ry[...]

    mine, theirs = pl.multiple_of(core * BLK, BLK), pl.multiple_of(other * BLK, BLK)
    half = pl.ds(mine, BLK)

    def put(m, value):
        g[m] = value
        send(g.at[m, pl.ds(theirs, BLK)], gc.at[m], GC + m, mate)

    m1, m2 = own[7, 0], own[7, 1]
    m1s, m1t = split(m1), split(m1.T)
    n1t, n2t, n1ct = ((nt[0, k], nt[1, k]) for k in range(3))
    n2s = (nn[0], nn[1])
    put(0, dot3(n1t, m1s))
    mc = dot3(m1s, c_split)
    mcs = split(mc)
    minus = lambda v: tuple(-u for u in v)
    put(1, dot3(join((m1t, n1t), 1), join((n2s, minus(mcs)), 0)))
    p2 = mc - m2
    put(2, dot3(join((n2t, split(mc.T), n1ct), 1), join((split(-p2), minus(n2s), mcs), 0)))
    p1_out[...] = -m1
    p2_out[...] = p2
    planes = (("y", "z", "x"), ("z", "x", "y"), ("x", "y", "z"))

    def shifted(m, i, j, k):
        return at(**dict(zip(planes[m], (i, j, k))))

    def piece(m, i, j):
        u, v, _ = planes[m]
        index = lax.rem(pos[u] + i, 4) * 4 + lax.rem(pos[v] + j, 4)
        return pl.ds(pl.multiple_of(mine + index * 8, 8), 8)

    order = sorted(
        ((i, j) for i in range(4) for j in range(4) if (i, j) != (0, 0)),
        key=lambda q: -(1.01 * min(q[0], 4 - q[0]) + min(q[1], 4 - q[1])),
    )
    for m in range(3):
        arrived(gc.at[m], GC + m)
        g[m, half] += gc[m]
        for i, j in order:
            send(g.at[m, piece(m, i, j)], r1.at[m, i * 4 + j], R1 + m, shifted(m, i, j, 0), 2)
    for m in range(3):
        arrived(r1.at[m, 1:16], R1 + m)
        total = g[m, piece(m, 0, 0)]
        for q in range(1, 16):
            total += r1[m, q]
        slot = pos[planes[m][2]]
        zs[m, slot] = total
        for k in (2, 1, 3):
            send(zs.at[m, slot], zs.at[m, slot], R2 + m, shifted(m, 0, 0, k), 2)
    for m in range(3):
        arrived(zs.at[m, 1:4], R2 + m)
        at_piece = piece(m, 0, 0)
        res[m, at_piece] = const[m, at_piece] + ((zs[m, 0] + zs[m, 1]) + (zs[m, 2] + zs[m, 3]))
        for i, j in order:
            send(res.at[m, at_piece], res.at[m, at_piece], R3 + m, shifted(m, i, j, 0), 2)
    for m in range(3):
        arrived(res.at[m, 0:120], R3 + m)
        send(res.at[m, half], res.at[m, half], GF + m, mate)
    for m, out in enumerate((b1_out, bc_out, b2_out)):
        arrived(res.at[m, pl.ds(theirs, BLK)], GF + m)
        out[...] = res[m]

    sent(give, 0)
    rows = 2 * BLK + 12 * XR + 2 * XR + 14 * YR + 6 * BLK
    sent(a.at[0:4, 0 : rows // 16], 1)
    sent(fac.at[0, 0 : 3 * (120 + 24 + 120)], 2)


def per_device(inverse, pattern, first, second, rows1, rows2, coupling, diag1, diag2):
    any_, vmem = pl.BlockSpec(memory_space=pl.ANY), pl.BlockSpec(memory_space=pltpu.VMEM)
    V = pltpu.VMEM
    outs = pl.pallas_call(
        kernel,
        out_shape=[V((BLK, W), F32)] * 2 + [V((W, W), F32)] * 3,
        in_specs=[pl.BlockSpec(memory_space=pltpu.HBM)] * 9,
        out_specs=[vmem] * 5,
        scratch_shapes=[
            V((8, 256, 1024), F32),
            V((2, 1024, W), F32),
            V((1024, 2 * W), BF16),
            V((1024, 2 * W), BF16),
            V((8, 2, BLK, W), F32),
            V((8, 2, BLK, W), F32),
            V((8, 2, BLK, W), F32),
            V((2, BLK, W), F32),
            V((2, 3, W, BLK), BF16),
            V((2, BLK, W), BF16),
            V((2, 2, XR, W), F32),
            V((2, 2, 2, XR, W), F32),
            V((2, XR, W), F32),
            V((4, 2, YR, W), F32),
            V((2, YR, W), F32),
            V((2, 2, YR, W), F32),
            V((3, W, W), F32),
            V((3, BLK, W), F32),
            V((3, 16, 8, W), F32),
            V((3, 4, 8, W), F32),
            V((3, W, W), F32),
            V((3, W, W), F32),
            V((W, W), F32),
            V((64,), jnp.int32),
            V((64,), jnp.int32),
            pltpu.SMEM((8, 16), jnp.int32),
            pltpu.SemaphoreType.DMA((3,)),
            pltpu.SemaphoreType.DMA((NSEM,)),
            pltpu.SemaphoreType.DMA((6,)),
            pltpu.SemaphoreType.DMA((8,)),
            pltpu.SemaphoreType.REGULAR((ROUNDS,)),
        ],
        compiler_params=pltpu.CompilerParams(
            collective_id=0, has_side_effects=True, vmem_limit_bytes=60 * 2**20
        ),
    )(inverse, pattern.T, first, second, rows1, rows2, coupling, diag1, diag2)
    return pl.pallas_call(
        hand_over,
        out_shape=[jax.ShapeDtypeStruct(o.shape, o.dtype) for o in outs],
        in_specs=[vmem] * 5,
        out_specs=[any_] * 5,
        scratch_shapes=[pltpu.SemaphoreType.DMA((5,))],
    )(*[pltpu.with_memory_space_constraint(o, pltpu.VMEM) for o in outs])


def hand_over(*refs):
    sem = refs[-1]
    copies = [pltpu.make_async_copy(refs[i], refs[5 + i], sem.at[i]) for i in (2, 3, 4, 0, 1)]
    for copy in copies:
        copy.start()
    for copy in copies:
        copy.wait()


def solution(mesh):
    return jax.shard_map(
        per_device,
        mesh=mesh,
        in_specs=(
            P("row", "col"), P("row", "col"), P("col", None), P("col", None),
            P(), P(), P(), P(), P(),
        ),
        out_specs=(P(("row", "col"), None), P(("row", "col"), None), P(), P(), P()),
        check_vma=False,
    )
```
